128 devices in a mesh: row: 16 (over y_lo, x, core), col: 8 (over z, y_hi).
Axes of the slice: x: 4, y: 4 (y_hi: 2, y_lo: 2; y = y_hi * 2 + y_lo), z: 4, core: 2. Of those that a mesh axis runs over, the one named last changes fastest.
Arguments:
- spectra: bfloat16 [32, 4096, 512], P(None, ('row', 'col')), may hold values from -6 to 6
- quality: int32 [4096], P(('row', 'col')), may hold values 0 or 1
- tile_mask: int32 [32, 32], replicated, may hold values 0 or 1
Outputs:
- correlations: bfloat16 [64, 4096, 4096], P(None, 'row', 'col')
The draws below stay inside these ranges and needn't reach their ends.
All inputs are finite; a program needn't handle non-finite values. No bound on the sum of `quality` on one device may be relied on, other than what follows from the above.
Results may differ from the reference program's by a relative error of at most 0.0066.
Values may be sent and summed in bfloat16 or wider, within the bound.
A program may use at most 192 MiB of HBM per device.

```python
import math
import jax
import jax.numpy as jnp
from jax import lax

C = 4096
F = 32
LAGS = 64
W = 256
BLK = 128


def with_ends(drawn, stream_key, smallest, largest):
    extent = drawn.shape
    place = [jax.random.randint(jax.random.fold_in(stream_key, axis), (), 0, extent[axis]) for axis in range(len(extent))]
    drawn = drawn.at[tuple(place)].set(smallest)
    longest = extent.index(max(extent))
    place[longest] = (place[longest] + 1) % extent[longest]
    return drawn.at[tuple(place)].set(largest)


def block_levels(rng, shape, shards, low, top_value):
    loudness = 1.0
    for dim, parts in shards:
        draws = jax.random.uniform(jax.random.fold_in(jax.random.fold_in(rng, 6), dim), (parts,), jnp.float32, low / len(shards), top_value / len(shards))
        loudness = loudness * jnp.repeat(jnp.exp(draws), shape[dim] // parts).reshape((-1,) + (1,) * (len(shape) - 1 - dim))
    return loudness


def noise(stream_key, extent, width, reach, pieces=(), kind=jnp.bfloat16):
    drawn = width * jax.random.normal(stream_key, extent, jnp.float32)
    if pieces:
        drawn = drawn * block_levels(stream_key, extent, pieces, -0.22, 0.18)
    return jnp.clip(drawn, -reach, reach).astype(kind)


def setup_inputs(seed: int = 0) -> dict:
    streams_of = jax.random.split(jax.random.key(seed), 4)
    spectra = noise(streams_of[0], (F, C, 2 * W), 1.0, 6.0, ((1, 128),))
    quality = with_ends((jax.random.randint(streams_of[1], (C,), 0, 8) < 7).astype(jnp.int32), jax.random.fold_in(streams_of[1], 1), 0, 1)
    tile_mask = with_ends((jax.random.randint(streams_of[2], (C // BLK, C // BLK), 0, 4) < 3).astype(jnp.int32), jax.random.fold_in(streams_of[2], 1), 0, 1)
    return dict(spectra=spectra, quality=quality, tile_mask=tile_mask)


def whiten(spectra, quality):
    values = spectra.astype(jnp.float32)
    half_width = values.shape[2] // 2
    real_part = values[:, :, :half_width]
    imag_part = values[:, :, half_width:]
    energy = real_part * real_part + imag_part * imag_part
    mean_energy = lax.optimization_barrier(jnp.mean(energy, axis=0, keepdims=True))
    factor = quality.astype(jnp.float32)[None, :, None] / jnp.sqrt(energy + mean_energy + 1e-06)
    return jnp.concatenate([real_part * factor, imag_part * factor], axis=2).astype(jnp.bfloat16)

def make_basis():
    lag_offset = jnp.arange(LAGS, dtype=jnp.float32) - LAGS / 2
    frequency = jnp.arange(F, dtype=jnp.float32) + 1.0
    angles = 2.0 * math.pi * frequency[None, :] * lag_offset[:, None] / (2.0 * LAGS)
    return jnp.stack([jnp.cos(angles), -jnp.sin(angles)], axis=1).astype(jnp.bfloat16)

def reference(spectra, quality, tile_mask):
    white = whiten(spectra, quality)
    half_width = white.shape[2] // 2
    turned = jnp.concatenate([-white[:, :, half_width:], white[:, :, :half_width]], axis=2)
    both_parts = jnp.concatenate([white, turned], axis=1).astype(jnp.float32)
    lag_basis = make_basis().astype(jnp.float32)
    norm_scale = 1.0 / math.sqrt(W * F)
    col_tiles = C // BLK

    def one_block(block_index):
        rows_here = lax.dynamic_slice_in_dim(white, block_index * BLK, BLK, 1).astype(jnp.float32)
        cross_spec = jnp.einsum('fiw,fjw->fij', rows_here, both_parts).astype(jnp.bfloat16)
        cross_spec = cross_spec.astype(jnp.float32).reshape(F, BLK, 2, C)
        lagged = jnp.einsum('lpf,fipj->lij', lag_basis, cross_spec)
        mask_tiles = lax.dynamic_index_in_dim(tile_mask, block_index, 0, keepdims=False).astype(jnp.float32)
        mask_row = jnp.broadcast_to(mask_tiles[:, None], (col_tiles, BLK)).reshape(C)
        return (lagged * norm_scale * mask_row[None, None, :]).astype(jnp.bfloat16)
    blocks = lax.map(one_block, jnp.arange(C // BLK).astype(jnp.int32))
    return jnp.transpose(blocks, (1, 0, 2, 3)).reshape(LAGS, C, C)
```

```python
import functools
import math

import jax
import jax.numpy as jnp
import numpy as np
from jax import lax
from jax.experimental import pallas as pl
from jax.experimental.pallas import tpu as pltpu
from jax.sharding import PartitionSpec as P

F = 32
LAGS = 64
HALF = LAGS // 2
W = 256
BLK = 128
CH = 32
NC = 8
NF = F // NC
MESH = pl.DeviceIdType.MESH

ROW = {'E1': (2, 4), 'E3': (2, 4), 'P0': (4, 12), 'P1': (11, 9), 'E2': (11, 6), 'P3': (15, 8), 'P2': (15, 7)}
NAMES = {'E0': 'a0', 'P0': 'a1', 'P1': 'a2', 'E1': 'b0', 'E3': 'b1', 'E2': 'b2', 'P3': 'y0', 'P2': 'y1'}
PIECE = {n: p for p, n in NAMES.items()}
COL = {'a0': (5, ((0, 2, 4, 5), (8, 6, 9, 10))), 'a1': (9, ((6, 11, 12, 13), (22, 19, 15, 18))),
       'a2': (6, ((13, 17, 18, 19), (21, 18, 20, 23))), 'b0': (8, ((0, 8, 7, 6), (9, 11, 10, 7))),
       'b1': (10, ((0, 6, 5, 4), (13, 12, 10, 12))), 'b2': (4, ((14, 23, 22, 21), (26, 29, 26, 22))),
       'y0': (6, ((17, 9, 11, 9), (5, 7, 8, 7))), 'y1': (6, ((17, 21, 23, 21), (17, 19, 22, 19)))}
MUL = (29, 5)
ENTRY = {0: ('y0', 'y1'), 1: ('a0', 'a2'), 2: ('a1', 'b1'), 3: ('b0', 'b2')}
TICKS = MUL[0] + (MUL[1] * (NC - 1)) // 4 + 1


def whiten(spectra, quality):
    values = spectra.astype(jnp.float32)
    half_width = values.shape[2] // 2
    real_part = values[:, :, :half_width]
    imag_part = values[:, :, half_width:]
    energy = real_part * real_part + imag_part * imag_part
    mean_energy = jnp.mean(energy, axis=0, keepdims=True)
    factor = quality.astype(jnp.float32)[None, :, None] / jnp.sqrt(energy + mean_energy + 1e-06)
    return jnp.concatenate([real_part * factor, imag_part * factor], axis=2).astype(jnp.bfloat16)


def any_of(q, places):
    hit = q < 0
    for place in places:
        hit = hit | (q == place)
    return hit


def pick(mirror, q, table):
    value = jnp.int32(table[0][0])
    for m in range(2):
        for place in range(4):
            value = jnp.where((mirror == m) & (q == place), table[m][place], value)
    return value


def gather_kernel(white, cross, rowb, colb, passb, local_sem, row_sem, row2_sem, pass_sem, col_sem, sib_sem,
                  srow_sem, sy_sem, sr_sem, scol_sem):
    row, col = lax.axis_index("row"), lax.axis_index("col")
    core, x, y_lo = row % 2, (row // 2) % 4, row // 8
    z, y_hi = col // 2, col % 2
    y = y_hi * 2 + y_lo

    def at(xx, yy, zz, cc):
        return {"row": (yy % 2) * 8 + xx * 2 + cc, "col": zz * 2 + yy // 2}

    x_up, x_dn = at((x + 1) % 4, y, z, core), at((x + 3) % 4, y, z, core)
    y_up, y_dn = at(x, (y + 1) % 4, z, core), at(x, (y + 3) % 4, z, core)
    z_up, z_dn = at(x, y, (z + 1) % 4, core), at(x, y, (z + 3) % 4, core)
    sibling = at(x, y, z, 1 - core)
    pair = at(x, y_hi * 2 + 1 - y_lo, z, core)
    other = at(x, (y + 3 + 2 * y_lo) % 4, z, core)

    q = (x + 4 - col % 4) % 4
    mirror = (y_lo + 2 - col // 4) % 2
    k = y_lo * 4 + x
    is_root = k == col
    feeds = (z == k // 2) & (y_hi != k % 2)

    def ident(piece):
        half = y_hi if piece[0] == 'E' else 1 - y_hi
        return ((z + int(piece[1])) % 4) * 2 + half

    ids = {p: ident(p) for p in NAMES}

    def chunk(g):
        return pl.ds(g * NF, NF)

    def remote(src, dst, send, recv, to):
        pltpu.make_async_remote_copy(src, dst, send, recv, device_id=to, device_id_type=MESH).start()

    def row_send(slot, piece, g, to):
        part = rowb.at[ids[piece], chunk(g)]
        remote(part, part, srow_sem.at[slot], row_sem.at[ids[piece], g], to)

    def col_send(src, slot, way, piece, g, to):
        dst = colb.at[core * 8 + ids[piece], chunk(g)]
        remote(dst if src is None else src, dst, scol_sem.at[slot, way], col_sem.at[ids[piece], g], to)

    def sib_send(src, slot, piece, g):
        dst = colb.at[core * 8 + ids[piece], chunk(g)]
        remote(dst if src is None else src, dst, scol_sem.at[slot, 3], sib_sem.at[ids[piece], g], sibling)

    def done(ref, sem):
        pltpu.make_async_copy(ref, ref, sem).wait()

    slots = {n: i for i, n in enumerate(PIECE)}
    own = pltpu.make_async_copy(white, rowb.at[ids['E0']], local_sem)
    own.start()
    barrier = pltpu.get_barrier_semaphore()
    for peer in (x_up, x_dn, y_up, y_dn, z_up, z_dn, sibling):
        pl.semaphore_signal(barrier, inc=1, device_id=peer, device_id_type=MESH)
    pl.semaphore_wait(barrier, 7)
    own.wait()

    def root_step(piece, g):
        name = NAMES[piece]
        src = rowb.at[ids[piece], chunk(g)]
        if name[0] == 'a':
            col_send(src, slots[name], 0, piece, g, x_up)
        if name[0] == 'b':
            col_send(src, slots[name], 1, piece, g, x_dn)
        sib_send(src, slots[name], piece, g)
        pltpu.make_async_copy(src, colb.at[core * 8 + ids[piece], chunk(g)], col_sem.at[ids[piece], g]).start()

    def first(g, carry):
        row_send(0, 'E0', g, z_up)
        row_send(1, 'E0', g, z_dn)

        @pl.when(is_root)
        def _():
            root_step('E0', g)

        return carry

    lax.fori_loop(0, NC, first, 0)

    hf = NF // 2

    def y_own(g):
        src = rowb.at[ids['E0'], pl.ds(g * NF, hf)]
        remote(src, passb.at[0, g], sy_sem.at[0], pass_sem.at[0, g], y_up)
        src = rowb.at[ids['E0'], pl.ds(g * NF + hf, hf)]
        remote(src, passb.at[1, g], sy_sem.at[1], pass_sem.at[1, g], y_dn)

    low_id = z * 2 + (y + 3) % 4 // 2
    high_id = z * 2 + (y + 1) % 4 // 2

    def y_pass(g):
        done(passb.at[0, g], pass_sem.at[0, g])
        remote(passb.at[0, g], rowb.at[low_id, pl.ds(g * NF, hf)], sy_sem.at[2], row_sem.at[low_id, g], y_up)
        done(passb.at[1, g], pass_sem.at[1, g])
        remote(passb.at[1, g], rowb.at[high_id, pl.ds(g * NF + hf, hf)], sy_sem.at[3], row2_sem.at[g], y_dn)

    def row_step(piece, g):
        if piece == 'P0':
            done(rowb.at[ids[piece], pl.ds(g * NF, hf)], row_sem.at[ids[piece], g])
            done(rowb.at[ids[piece], pl.ds(g * NF + hf, hf)], row2_sem.at[g])
        else:
            done(rowb.at[ids[piece], chunk(g)], row_sem.at[ids[piece], g])
        if piece == 'E3':
            row_send(2, piece, g, z_up)
        if piece == 'P0':
            row_send(3, piece, g, z_up)
            row_send(4, piece, g, z_dn)
        if piece == 'P1':
            row_send(5, piece, g, z_dn)

        @pl.when(is_root)
        def _():
            root_step(piece, g)

        if piece in ('E3', 'E2'):
            @pl.when(feeds)
            def _():
                dst = colb.at[core * 8 + ids[piece], chunk(g)]
                remote(rowb.at[ids[piece], chunk(g)], dst, sr_sem.at[0 if piece == 'E3' else 1],
                       col_sem.at[ids[piece], g], other)

    on_root_row = mirror == 0
    ways = {}
    for name in slots:
        up = on_root_row & any_of(q, (1, 2)) & (name[0] == 'a')
        down = on_root_row & any_of(q, (3, 2)) & (name[0] == 'b')
        over = jnp.where(on_root_row, any_of(q, [p for p in (1, 2, 3) if name in ENTRY[p]]),
                         any_of(q, (1, 2, 3)) & (name[0] == 'y'))
        enters = [p for p in range(4) if name in ENTRY[p]][0]
        order = ENTRY[enters].index(name)
        mirrored = mirror == 1
        full = mirrored & (q == enters)
        up_half = mirrored & (q == (enters + 1) % 4)
        down_half = mirrored & (q == (enters + 3) % 4)
        ways[name] = (up | full, up_half, down | full, down_half, over, order)

    def col_step(name, g):
        piece = PIECE[name]
        slot = slots[name]
        done(colb.at[core * 8 + ids[piece], chunk(g)], col_sem.at[ids[piece], g])
        up, up_half, down, down_half, over, order = ways[name]

        @pl.when(up | (up_half & (g % 2 == order)))
        def _():
            col_send(None, slot, 0, piece, g, x_up)

        @pl.when(down | (down_half & (g % 2 != order)))
        def _():
            col_send(None, slot, 1, piece, g, x_dn)

        @pl.when(over)
        def _():
            col_send(None, slot, 2, piece, g, pair)

        sib_send(None, slot, piece, g)

    def multiply(g):
        @pl.when(is_root)
        def _():
            for p in NAMES:
                done(colb.at[core * 8 + ids[p], chunk(g)], col_sem.at[ids[p], g])

        for p in NAMES:
            done(colb.at[(1 - core) * 8 + ids[p], chunk(g)], sib_sem.at[ids[p], g])

        def two_bins(h, carry):
            parts = []
            for e in range(2):
                f = g * NF + h * 2 + e
                lhs = rowb[:, f].reshape(8 * CH, 2 * W)
                turned = jnp.concatenate([lhs[:, W:], -lhs[:, :W]], axis=1)
                rhs = colb[:, f].reshape(16 * CH, 2 * W)
                parts.append(lax.dot_general(jnp.concatenate([lhs, turned], axis=0), rhs, (((1,), (1,)), ((), ())),
                                             preferred_element_type=jnp.float32))
            for c in range(2):
                both = [p[c * 256:(c + 1) * 256].reshape(32, 8, 512) for p in parts]
                cross[c, :, g * (NF // 2) + h] = jnp.concatenate(both, axis=1).astype(jnp.bfloat16)
            return carry

        lax.fori_loop(0, NF // 2, two_bins, 0)

    not_root = jnp.logical_not(is_root)
    always = row >= 0
    jobs = [(y_own, 0, 8, always), (y_pass, 2, 8, always)]
    for piece in ('E3', 'E1', 'P0', 'P1', 'E2', 'P3', 'P2'):
        jobs.append((functools.partial(row_step, piece), *ROW[piece], always))
    for name in ('a0', 'b0', 'y0', 'b1', 'a1', 'y1', 'a2', 'b2'):
        rate, table = COL[name]
        jobs.append((functools.partial(col_step, name), pick(mirror, q, table), rate, not_root))
    jobs.append((multiply, *MUL, always))

    def tick(t, state):
        after = []
        for (act, start, rate, on), g in zip(jobs, state):
            due = on & (g < NC) & (t >= start + (rate * g) // 4)

            @pl.when(due)
            def _(act=act, g=g):
                act(g)

            after.append(g + due.astype(jnp.int32))
        return tuple(after)

    lax.fori_loop(0, TICKS, tick, tuple(jnp.int32(0) for _ in jobs))

    whole = rowb.at[0]
    half_piece = rowb.at[0, pl.ds(0, F // 2)]
    for i in range(6):
        done(whole, srow_sem.at[i])
    for i in range(4):
        done(half_piece, sy_sem.at[i])

    @pl.when(feeds)
    def _():
        done(whole, sr_sem.at[0])
        done(whole, sr_sem.at[1])

    for name in slots:
        up, up_half, down, down_half, over, _ = ways[name]
        slot = slots[name]
        for way, full, part, letter in ((0, up, up_half, 'a'), (1, down, down_half, 'b')):
            @pl.when(jnp.where(is_root, name[0] == letter, full))
            def _(slot=slot, way=way):
                done(whole, scol_sem.at[slot, way])

            @pl.when(not_root & part)
            def _(slot=slot, way=way):
                done(half_piece, scol_sem.at[slot, way])

        @pl.when(not_root & over)
        def _(slot=slot):
            done(whole, scol_sem.at[slot, 2])

        done(whole, scol_sem.at[slot, 3])


def gather_cross(white):
    piece = (F, CH, 2 * W)
    return pl.pallas_call(
        gather_kernel,
        out_shape=pltpu.VMEM((2, 32, F // 2, 16, 512), jnp.bfloat16),
        in_specs=[pl.BlockSpec(memory_space=pltpu.VMEM)],
        out_specs=pl.BlockSpec(memory_space=pltpu.VMEM),
        scratch_shapes=[
            pltpu.VMEM((8, *piece), jnp.bfloat16),
            pltpu.VMEM((16, *piece), jnp.bfloat16),
            pltpu.VMEM((2, NC, NF // 2, CH, 2 * W), jnp.bfloat16),
            pltpu.SemaphoreType.DMA,
            pltpu.SemaphoreType.DMA((8, NC)),
            pltpu.SemaphoreType.DMA((NC,)),
            pltpu.SemaphoreType.DMA((2, NC)),
            pltpu.SemaphoreType.DMA((8, NC)),
            pltpu.SemaphoreType.DMA((8, NC)),
            pltpu.SemaphoreType.DMA((6,)),
            pltpu.SemaphoreType.DMA((4,)),
            pltpu.SemaphoreType.DMA((2,)),
            pltpu.SemaphoreType.DMA((8, 4)),
        ],
        compiler_params=pltpu.CompilerParams(collective_id=0, has_side_effects=True, vmem_limit_bytes=40 << 20),
        name="gather_cross",
    )(white)


def lag_matrices():
    lag = np.arange(HALF + 1, dtype=np.float32)
    frequency = np.arange(F, dtype=np.float32) + np.float32(1.0)
    angles = np.float32(2.0 * math.pi) * frequency[None, :] * lag[:, None] / np.float32(2.0 * LAGS)
    eye = np.eye(8, dtype=np.float32)
    return [np.kron(m, eye).astype(jnp.bfloat16) for m in (np.cos(angles), -np.sin(angles))]


def lag_kernel(mask, cross, even_mat, odd_mat, out):
    cols = out.shape[2]
    step = pl.program_id(0)
    tile_row = lax.axis_index("row") * 2 + step // 8
    tile_col = lax.axis_index("col") * (cols // BLK)
    scale = jnp.concatenate(
        [jnp.full((1, BLK), mask[tile_row, tile_col + t].astype(jnp.float32) * (1.0 / math.sqrt(W * F)), jnp.float32)
         for t in range(cols // BLK)], axis=1)
    even, odd = [], []
    for h in range(2):
        at = step * 2 + h
        even.append(jnp.dot(even_mat[...], cross[0, at].reshape(F * 8, cols), preferred_element_type=jnp.float32))
        odd.append(jnp.dot(odd_mat[...], cross[1, at].reshape(F * 8, cols), preferred_element_type=jnp.float32))
    for m in range(HALF + 1):
        e = [v[m * 8:m * 8 + 8] for v in even]
        o = [v[m * 8:m * 8 + 8] for v in odd]
        if m < HALF:
            out[HALF + m] = (jnp.concatenate([a + b for a, b in zip(e, o)], 0) * scale).astype(out.dtype)
        if m > 0:
            out[HALF - m] = (jnp.concatenate([a - b for a, b in zip(e, o)], 0) * scale).astype(out.dtype)


def lag_transform(cross, tile_mask):
    rows, cols = 256, 512
    even_mat, odd_mat = lag_matrices()
    return pl.pallas_call(
        lag_kernel,
        grid=(rows // 16,),
        in_specs=[
            pl.BlockSpec(memory_space=pltpu.SMEM),
            pl.BlockSpec(memory_space=pltpu.VMEM),
            pl.BlockSpec(even_mat.shape, lambda i: (0, 0)),
            pl.BlockSpec(odd_mat.shape, lambda i: (0, 0)),
        ],
        out_specs=pl.BlockSpec((LAGS, 16, cols), lambda i: (0, i, 0)),
        out_shape=jax.ShapeDtypeStruct((LAGS, rows, cols), jnp.bfloat16),
        compiler_params=pltpu.CompilerParams(vmem_limit_bytes=30 << 20),
        name="lag_transform",
    )(tile_mask, cross, even_mat, odd_mat)


def per_device(spectra, quality, tile_mask):
    cross = gather_cross(whiten(spectra, quality))
    return lag_transform(cross, tile_mask)


def solution(mesh):
    placed = (P(None, ("row", "col"), None), P(("row", "col")), P())
    return jax.shard_map(
        per_device, mesh=mesh, in_specs=placed, out_specs=P(None, "row", "col"), check_vma=False
    )
```

```python
import functools
import math

import jax
import jax.numpy as jnp
import numpy as np
from jax import lax
from jax.experimental import pallas as pl
from jax.experimental.pallas import tpu as pltpu
from jax.sharding import PartitionSpec as P

F = 32
LAGS = 64
HALF = LAGS // 2
W = 256
BLK = 128
CH = 32
MESH = pl.DeviceIdType.MESH

NAMES = {'E1': 'a0', 'P0': 'a1', 'E2': 'a2', 'E0': 'b0', 'E3': 'b1', 'P3': 'b2', 'P1': 'y0', 'P2': 'y1'}
ENTRY = {0: ('y0', 'y1'), 1: ('a0', 'a2'), 2: ('b1', 'a1'), 3: ('b0', 'b2')}
NC = 8
BEFORE, BETWEEN = 37, 5
ORDER = (
    (8389120, 8675344, 12846097, 795682, 9446947, 13109268, 1321509, 10234918, 1598999, 1867856, 13664864, 25461841,
     21523011, 134217328, 134217727, 134217727, 134217727, 134217727, 134217727, 134217727, 134217727, 134217727,
     134217727, 134217727, 134217727, 134217727, 134217727, 134217727, 134217727, 134217727, 134217727, 134217727,
     134217727, 134217727, 134217727, 134217727, 134217727, 29657171, 134217727, 134217727, 134217727, 134217727,
     22070326, 134014007, 134217727, 134217727, 134217727, 22579797, 26011206, 134217727, 134217727, 134217727,
     18656868, 134217332, 134217727, 134217727, 134217727, 134015589, 134217727, 134217727, 134217727, 134217727,
     134016102, 134217727, 134217727, 134217727, 134217727, 134016615, 134217727, 134217727, 134217727, 134217727),
    (4194816, 4481056, 12846113, 8922240, 812176, 46155283, 9447553, 13371569, 9710225, 58786994, 9972741, 6096563,
     47212583, 59049990, 47480912, 1862290, 34958401, 21283042, 35221058, 17613366, 14487232, 38634066, 50913507,
     21874848, 38897220, 22070501, 42305649, 51700966, 22400661, 26035398, 30181974, 42852551, 54585431, 134217727,
     134217727, 134217727, 134217727, 18401430, 134062833, 134217727, 134217727, 134217727, 18664100, 39691381,
     134217458, 134217727, 134217727, 43314278, 31248115, 55437478, 134217727, 134217727, 134064295, 134217727,
     134217727, 134217727, 134217727, 134064885, 134217727, 134217727, 134217727, 134217727, 134065398, 134217727,
     134217727, 134217727, 134217727, 134065911, 134217727, 134217727, 134217727, 134217727),
    (4194816, 4481056, 12846113, 8922288, 4982449, 46727203, 37767188, 46949380, 33835541, 5769908, 47522342,
     13389335, 47713410, 58753104, 1928835, 13699137, 25264353, 38306897, 17613505, 59271813, 29402306, 21857926,
     59575921, 38578372, 51759158, 29919330, 51932832, 60089941, 22646420, 54608614, 39118917, 26059495, 42503255,
     134078674, 134217727, 134217727, 134217727, 26560100, 39381575, 55372902, 31248036, 134217457, 55914196,
     43625637, 134217458, 134217727, 134217727, 63786711, 134217727, 134217727, 134217727, 134217727, 134217460,
     134217727, 134217727, 134217727, 134217727, 134217461, 134217727, 134217727, 134217727, 134217727, 134081783,
     134217727, 134217727, 134217727, 134217727, 134217727, 134217727, 134217727, 134217727, 134217727),
    (46137856, 12591136, 4473521, 46686722, 13116450, 9266691, 9529363, 13371412, 9792128, 1425429, 10054800,
     48038422, 13643303, 38126086, 16818368, 34082357, 59278017, 21282947, 14189762, 51167876, 21570627, 14452932,
     51710691, 35244144, 51947106, 35506757, 29724244, 26027750, 60613840, 54831776, 18394260, 63022195, 134217727,
     134217727, 134217727, 134217727, 134217727, 39095969, 30453348, 134217457, 134217727, 134217727, 26559699,
     63547509, 134217727, 134217727, 134217727, 42789990, 31248085, 63810710, 134217727, 134217727, 64073380,
     134217727, 134217727, 134217727, 134217727, 64309911, 134217727, 134217727, 134217727, 134217727, 64573094,
     134217727, 134217727, 134217727, 134217727, 134217463, 134217727, 134217727, 134217727, 134217727),
    (4194816, 8659488, 12846128, 58737682, 9184771, 9447649, 13109424, 46418453, 1376482, 13388822, 46681623,
     33932806, 59801680, 17088519, 60104883, 47219793, 25494580, 60360259, 60648018, 38068356, 29657171, 62941878,
     48015458, 29912197, 63245504, 14453333, 18394258, 35513459, 63800419, 22857921, 54585415, 134037748, 134217727,
     134217727, 134217727, 134217727, 134217727, 54848101, 134038261, 134217727, 134217727, 134217727, 51440742,
     27084022, 134063223, 134217727, 134217727, 38635255, 134063779, 134217727, 134217727, 134217727, 43100357,
     55921350, 52276390, 56446613, 134217364, 134217727, 134217727, 134217727, 134217727, 134217727, 134217366,
     134217727, 134217727, 134217727, 134217727, 134217367, 134217727, 134217727, 134217727, 134217727),
    (8389120, 4473360, 12846128, 795682, 33564195, 5261362, 13371616, 58993189, 9964161, 46489622, 6049332, 37752034,
     16818306, 1862322, 34457153, 17343072, 25544849, 46991427, 21523685, 29388468, 34983104, 47482963, 25758951,
     38330964, 29953718, 42066113, 42304597, 18132067, 48095859, 42526807, 18401475, 51463922, 30707301, 26814195,
     51767414, 31248036, 134062289, 134217727, 134217727, 134217727, 134217727, 134217727, 51989237, 38882550,
     52252407, 55158421, 134217727, 134217727, 134217727, 134217727, 134217727, 134217727, 39692950, 134217428,
     134217727, 134217727, 134217727, 134217727, 134217727, 134217727, 134217727, 134217727, 134217430, 134217727,
     134217727, 134217727, 134217727, 134217431, 134217727, 134217727, 134217727, 134217727),
    (8389120, 8675344, 12846097, 795682, 4998706, 46147620, 9725444, 33645077, 10035205, 59097110, 6049332, 46727686,
     59277392, 17113607, 34170421, 17343072, 25455796, 34457155, 21594167, 59861616, 29664914, 50687108, 50973268,
     29919330, 51212006, 34924117, 22644967, 18163334, 35512436, 22857413, 42049606, 134217727, 134217727, 134217727,
     134217727, 134217727, 134217727, 54839494, 26552481, 63236679, 134217727, 134217727, 26840786, 63521910,
     134217727, 134217727, 134217727, 31248021, 55389347, 134217459, 134217727, 134217727, 43069172, 134217428,
     134217727, 134217727, 134217727, 55921397, 134217727, 134217727, 134217727, 134217727, 64875686, 134217430,
     134217727, 134217727, 134217727, 134065831, 134217727, 134217727, 134217727, 134217727),
    (4194816, 8659488, 12846128, 46154770, 9184771, 9447601, 13109472, 59001365, 5769906, 6055462, 33670183,
     21063174, 47259712, 59539975, 21282868, 47514178, 17613457, 47776996, 60065874, 34398261, 25788599, 60328531,
     22094902, 14536305, 29935236, 22381296, 54625413, 30182486, 54888177, 55150663, 30453348, 26545394, 38604405,
     63761510, 27101907, 55699575, 134037702, 134038229, 134217727, 134217727, 134217727, 134217727, 56174837,
     56463094, 134217378, 134217727, 134217727, 42856085, 134217727, 134217727, 134217727, 134217727, 134217380,
     134217727, 134217727, 134217727, 134217727, 39668886, 134217381, 134217727, 134217727, 134217727, 134217727,
     134217727, 134217727, 134217727, 134217727, 134217383, 134217727, 134217727, 134217727, 134217727),
)
NF = F // NC
ROWS = ('E3', 'E1', 'P0', 'P1', 'E2', 'P3', 'P2')
ITEMS = ('own', *ROWS, *sorted(NAMES.values()))
PIECE = {n: p for p, n in NAMES.items()}


def whiten(spectra, quality):
    values = spectra.astype(jnp.float32)
    half_width = values.shape[2] // 2
    real_part = values[:, :, :half_width]
    imag_part = values[:, :, half_width:]
    energy = real_part * real_part + imag_part * imag_part
    mean_energy = jnp.mean(energy, axis=0, keepdims=True)
    factor = quality.astype(jnp.float32)[None, :, None] / jnp.sqrt(energy + mean_energy + 1e-06)
    return jnp.concatenate([real_part * factor, imag_part * factor], axis=2).astype(jnp.bfloat16)


def any_of(q, places):
    hit = q < 0
    for place in places:
        hit = hit | (q == place)
    return hit


def gather_kernel(white, cross, rowb, colb, steps, local_sem, row_sem, col_sem, sib_sem, srow_sem, sr_sem, scol_sem):
    row, col = lax.axis_index("row"), lax.axis_index("col")
    core, x, y_lo = row % 2, (row // 2) % 4, row // 8
    z, y_hi = col // 2, col % 2
    y = y_hi * 2 + y_lo

    def at(xx, yy, zz, cc):
        return {"row": (yy % 2) * 8 + xx * 2 + cc, "col": zz * 2 + yy // 2}

    x_up, x_dn = at((x + 1) % 4, y, z, core), at((x + 3) % 4, y, z, core)
    z_up, z_dn = at(x, y, (z + 1) % 4, core), at(x, y, (z + 3) % 4, core)
    sibling = at(x, y, z, 1 - core)
    partner = at(x, (y + 2) % 4, z, core)
    pair = at(x, y_hi * 2 + 1 - y_lo, z, core)
    other = at(x, (y + 3 + 2 * y_lo) % 4, z, core)

    q = (x + 4 - col % 4) % 4
    mirror = (y_lo + 2 - col // 4) % 2
    place = mirror * 4 + q
    k = y_lo * 4 + x
    is_root = k == col
    not_root = jnp.logical_not(is_root)
    feeds = (z == k // 2) & (y_hi != k % 2)

    def ident(piece):
        half = y_hi if piece[0] == 'E' else 1 - y_hi
        return ((z + int(piece[1])) % 4) * 2 + half

    ids = {p: ident(p) for p in NAMES}

    def chunk(g):
        return pl.ds(g * NF, NF)

    def remote(src, dst, send, recv, to):
        pltpu.make_async_remote_copy(src, dst, send, recv, device_id=to, device_id_type=MESH).start()

    def row_send(slot, piece, g, to):
        part = rowb.at[ids[piece], chunk(g)]
        remote(part, part, srow_sem.at[slot], row_sem.at[ids[piece], g], to)

    def col_send(src, slot, way, piece, g, to):
        dst = colb.at[core * 8 + ids[piece], chunk(g)]
        remote(dst if src is None else src, dst, scol_sem.at[slot, way], col_sem.at[ids[piece], g], to)

    def sib_send(src, slot, piece, g):
        dst = colb.at[core * 8 + ids[piece], chunk(g)]
        remote(dst if src is None else src, dst, scol_sem.at[slot, 3], sib_sem.at[ids[piece], g], sibling)

    def done(ref, sem):
        pltpu.make_async_copy(ref, ref, sem).wait()

    slots = {n: i for i, n in enumerate(PIECE)}
    own = pltpu.make_async_copy(white, rowb.at[ids['E0']], local_sem)
    own.start()
    barrier = pltpu.get_barrier_semaphore()
    for peer in (x_up, x_dn, pair, other, z_up, z_dn, sibling, partner):
        pl.semaphore_signal(barrier, inc=1, device_id=peer, device_id_type=MESH)
    pl.semaphore_wait(barrier, 8)
    own.wait()

    def root_step(piece, g):
        name = NAMES[piece]
        src = rowb.at[ids[piece], chunk(g)]
        if name[0] == 'a':
            col_send(src, slots[name], 0, piece, g, x_up)
        if name[0] == 'b':
            col_send(src, slots[name], 1, piece, g, x_dn)
        sib_send(src, slots[name], piece, g)
        pltpu.make_async_copy(src, colb.at[core * 8 + ids[piece], chunk(g)], col_sem.at[ids[piece], g]).start()

    def first(g, carry):
        row_send(0, 'E0', g, z_up)
        row_send(1, 'E0', g, z_dn)

        @pl.when(is_root)
        def _():
            root_step('E0', g)

        return carry

    lax.fori_loop(0, NC, first, 0)

    def y_own(g):
        row_send(6, 'E0', g, partner)

    feed_slot = {'E' + PIECE[n][1]: i for i, n in enumerate(('y0', 'y1'))}

    def row_step(piece, g):
        done(rowb.at[ids[piece], chunk(g)], row_sem.at[ids[piece], g])
        if piece == 'E3':
            row_send(2, piece, g, z_up)
        if piece == 'P0':
            row_send(3, piece, g, z_up)
            row_send(4, piece, g, z_dn)
        if piece == 'P1':
            row_send(5, piece, g, z_dn)

        @pl.when(is_root)
        def _():
            root_step(piece, g)

        if piece in feed_slot:
            @pl.when(feeds)
            def _():
                dst = colb.at[core * 8 + ids[piece], chunk(g)]
                remote(rowb.at[ids[piece], chunk(g)], dst, sr_sem.at[feed_slot[piece]], col_sem.at[ids[piece], g], other)

    on_root_row = mirror == 0
    ways = {}
    for name in slots:
        up = on_root_row & any_of(q, (1, 2)) & (name[0] == 'a')
        down = on_root_row & any_of(q, (3, 2)) & (name[0] == 'b')
        over = jnp.where(on_root_row, any_of(q, [p for p in (1, 2, 3) if name in ENTRY[p]]),
                         any_of(q, (1, 2, 3)) & (name[0] == 'y'))
        enters = [p for p in range(4) if name in ENTRY[p]][0]
        order = ENTRY[enters].index(name)
        mirrored = mirror == 1
        full = mirrored & (q == enters)
        up_half = mirrored & (q == (enters + 1) % 4)
        down_half = mirrored & (q == (enters + 3) % 4)
        ways[name] = (up | full, up_half, down | full, down_half, over, order)

    def col_step(name, g):
        piece = PIECE[name]
        slot = slots[name]
        done(colb.at[core * 8 + ids[piece], chunk(g)], col_sem.at[ids[piece], g])
        up, up_half, down, down_half, over, order = ways[name]

        @pl.when(up | (up_half & (g % 2 == order)))
        def _():
            col_send(None, slot, 0, piece, g, x_up)

        @pl.when(down | (down_half & (g % 2 != order)))
        def _():
            col_send(None, slot, 1, piece, g, x_dn)

        @pl.when(over)
        def _():
            col_send(None, slot, 2, piece, g, pair)

        sib_send(None, slot, piece, g)

    def multiply(g):
        @pl.when(is_root)
        def _():
            for p in NAMES:
                done(colb.at[core * 8 + ids[p], chunk(g)], col_sem.at[ids[p], g])

        for p in NAMES:
            done(colb.at[(1 - core) * 8 + ids[p], chunk(g)], sib_sem.at[ids[p], g])

        def two_bins(h, carry):
            parts = []
            for e in range(2):
                f = g * NF + h * 2 + e
                lhs = rowb[:, f].reshape(8 * CH, 2 * W)
                turned = jnp.concatenate([lhs[:, W:], -lhs[:, :W]], axis=1)
                rhs = colb[:, f].reshape(16 * CH, 2 * W)
                parts.append(lax.dot_general(jnp.concatenate([lhs, turned], axis=0), rhs, (((1,), (1,)), ((), ())),
                                             preferred_element_type=jnp.float32))
            for c in range(2):
                both = [p[c * 256:(c + 1) * 256].reshape(32, 8, 512) for p in parts]
                cross[c, :, g * (NF // 2) + h] = jnp.concatenate(both, axis=1).astype(jnp.bfloat16)
            return carry

        lax.fori_loop(0, NF // 2, two_bins, 0)

    acts = [functools.partial(row_step, n) if n in ROWS else functools.partial(col_step, n) if n in PIECE
            else y_own for n in ITEMS]
    for i in range(len(ORDER[0])):
        word = jnp.int32(ORDER[0][i])
        for p in range(1, 8):
            word = jnp.where(place == p, ORDER[p][i], word)
        steps[i] = word

    def choose(item, g, low, high):
        if high - low == 1:
            acts[low](g)
            return
        middle = (low + high) // 2

        @pl.when(item < middle)
        def _():
            choose(item, g, low, middle)

        @pl.when(item >= middle)
        def _():
            choose(item, g, middle, high)

    def three(i, carry):
        def one(_, word):
            step = lax.rem(word, 512)
            item, g = lax.div(step, 16), lax.rem(step, 16)

            @pl.when(item < len(ITEMS))
            def _():
                choose(item, g, 0, len(ITEMS))

            return lax.div(word, 512)

        lax.fori_loop(0, 3, one, steps[i])
        return carry

    lax.fori_loop(0, BEFORE, three, 0)

    def with_multiply(g, carry):
        multiply(g)
        start = BEFORE + g * BETWEEN
        lax.fori_loop(start, start + BETWEEN, three, 0)
        return carry

    lax.fori_loop(0, NC - 1, with_multiply, 0)
    multiply(NC - 1)

    whole = rowb.at[0]
    half_piece = rowb.at[0, pl.ds(0, F // 2)]
    for i in range(7):
        done(whole, srow_sem.at[i])

    @pl.when(feeds)
    def _():
        done(whole, sr_sem.at[0])
        done(whole, sr_sem.at[1])

    for name in slots:
        up, up_half, down, down_half, over, _ = ways[name]
        slot = slots[name]
        for way, full, part, letter in ((0, up, up_half, 'a'), (1, down, down_half, 'b')):
            @pl.when(jnp.where(is_root, name[0] == letter, full))
            def _(slot=slot, way=way):
                done(whole, scol_sem.at[slot, way])

            @pl.when(not_root & part)
            def _(slot=slot, way=way):
                done(half_piece, scol_sem.at[slot, way])

        @pl.when(not_root & over)
        def _(slot=slot):
            done(whole, scol_sem.at[slot, 2])

        done(whole, scol_sem.at[slot, 3])


def gather_cross(white):
    piece = (F, CH, 2 * W)
    return pl.pallas_call(
        gather_kernel,
        out_shape=pltpu.VMEM((2, 32, F // 2, 16, 512), jnp.bfloat16),
        in_specs=[pl.BlockSpec(memory_space=pltpu.VMEM)],
        out_specs=pl.BlockSpec(memory_space=pltpu.VMEM),
        scratch_shapes=[
            pltpu.VMEM((8, *piece), jnp.bfloat16),
            pltpu.VMEM((16, *piece), jnp.bfloat16),
            pltpu.SMEM((len(ORDER[0]),), jnp.int32),
            pltpu.SemaphoreType.DMA,
            pltpu.SemaphoreType.DMA((8, NC)),
            pltpu.SemaphoreType.DMA((8, NC)),
            pltpu.SemaphoreType.DMA((8, NC)),
            pltpu.SemaphoreType.DMA((7,)),
            pltpu.SemaphoreType.DMA((2,)),
            pltpu.SemaphoreType.DMA((8, 4)),
        ],
        compiler_params=pltpu.CompilerParams(collective_id=0, has_side_effects=True, vmem_limit_bytes=40 << 20),
        name="gather_cross",
    )(white)


def lag_matrices():
    lag = np.arange(HALF + 1, dtype=np.float32)
    frequency = np.arange(F, dtype=np.float32) + np.float32(1.0)
    angles = np.float32(2.0 * math.pi) * frequency[None, :] * lag[:, None] / np.float32(2.0 * LAGS)
    eye = np.eye(8, dtype=np.float32)
    return [np.kron(m, eye).astype(jnp.bfloat16) for m in (np.cos(angles), -np.sin(angles))]


def lag_kernel(mask, cross, even_mat, odd_mat, out, buf, sem):
    rows, cols = out.shape[1], out.shape[2]
    wide = 256
    tile_row = lax.axis_index("row") * (rows // BLK)
    tile_col = lax.axis_index("col") * (cols // BLK)

    def copy(step):
        here = pl.ds(pl.multiple_of(step * 16, 16), 16)
        return pltpu.make_async_copy(buf.at[:, here], out.at[:, here], sem.at[step])

    def one(step, carry):
        here = pl.ds(pl.multiple_of(step * 16, 16), 16)
        for j in range(cols // wide):
            span = slice(j * wide, (j + 1) * wide)
            scale = jnp.concatenate(
                [jnp.full((1, BLK), mask[tile_row + step // 8, tile_col + t].astype(jnp.float32)
                          * (1.0 / math.sqrt(W * F)), jnp.float32)
                 for t in range(j * wide // BLK, (j + 1) * wide // BLK)], axis=1)
            even, odd = [], []
            for h in range(2):
                at = step * 2 + h
                even.append(jnp.dot(even_mat[...], cross[0, at, :, :, span].reshape(F * 8, wide),
                                    preferred_element_type=jnp.float32))
                odd.append(jnp.dot(odd_mat[...], cross[1, at, :, :, span].reshape(F * 8, wide),
                                   preferred_element_type=jnp.float32))
            for m in range(HALF + 1):
                e = [v[m * 8:m * 8 + 8] for v in even]
                o = [v[m * 8:m * 8 + 8] for v in odd]
                if m < HALF:
                    buf[HALF + m, here, span] = (
                        jnp.concatenate([a + b for a, b in zip(e, o)], 0) * scale).astype(out.dtype)
                if m > 0:
                    buf[HALF - m, here, span] = (
                        jnp.concatenate([a - b for a, b in zip(e, o)], 0) * scale).astype(out.dtype)
        copy(step).start()
        return carry

    lax.fori_loop(0, rows // 16, one, 0)

    def finish(step, carry):
        copy(step).wait()
        return carry

    lax.fori_loop(0, rows // 16, finish, 0)


def lag_transform(cross, tile_mask):
    rows, cols = 256, 512
    even_mat, odd_mat = lag_matrices()
    vmem = pl.BlockSpec(memory_space=pltpu.VMEM)
    return pl.pallas_call(
        lag_kernel,
        in_specs=[pl.BlockSpec(memory_space=pltpu.SMEM), vmem, vmem, vmem],
        out_specs=pl.BlockSpec(memory_space=pl.ANY),
        out_shape=jax.ShapeDtypeStruct((LAGS, rows, cols), jnp.bfloat16),
        scratch_shapes=[pltpu.VMEM((LAGS, rows, cols), jnp.bfloat16), pltpu.SemaphoreType.DMA((rows // 16,))],
        compiler_params=pltpu.CompilerParams(vmem_limit_bytes=30 << 20),
        name="lag_transform",
    )(tile_mask, cross, even_mat, odd_mat)


def per_device(spectra, quality, tile_mask):
    cross = gather_cross(whiten(spectra, quality))
    return lag_transform(cross, tile_mask)


def solution(mesh):
    placed = (P(None, ("row", "col"), None), P(("row", "col")), P())
    return jax.shard_map(
        per_device, mesh=mesh, in_specs=placed, out_specs=P(None, "row", "col"), check_vma=False
    )
```

```python
import functools
import math

import jax
import jax.numpy as jnp
import numpy as np
from jax import lax
from jax.experimental import pallas as pl
from jax.experimental.pallas import tpu as pltpu
from jax.sharding import PartitionSpec as P

F = 32
LAGS = 64
HALF = LAGS // 2
W = 256
BLK = 128
CH = 32
MESH = pl.DeviceIdType.MESH

NAMES = {'E1': 'a0', 'P0': 'a1', 'E2': 'a2', 'E0': 'b0', 'E3': 'b1', 'P3': 'b2', 'P1': 'y0', 'P2': 'y1'}
ENTRY = {0: ('y0', 'y1'), 1: ('a0', 'a2'), 2: ('b1', 'a1'), 3: ('b0', 'b2')}
NC = 16
BEFORE, BETWEEN = 73, 7
ORDER = (
    (8389120, 8651792, 8937489, 12846610, 1058339, 13117476, 1321509, 1584166, 13381159, 1847336, 13644329, 6837256,
     2373163, 13908012, 7625226, 2898990, 8150582, 16818188, 3441233, 14451808, 17605646, 17875512, 18130447,
     25719366, 22312020, 134012999, 134217727, 134217727, 134217727, 134217727, 134217727, 134217727, 134217727,
     134217727, 134217727, 134217727, 134217727, 134217727, 134217727, 134217727, 134217727, 134217727, 134217727,
     134217727, 134217727, 134217727, 134217727, 134217727, 134217727, 134217727, 134217727, 134217727, 134217727,
     134217727, 134217727, 134217727, 134217727, 134217727, 134217727, 134217727, 134217727, 134217727, 134217727,
     134217727, 134217727, 134217727, 134217727, 134217727, 134217727, 134217727, 134217727, 134217727, 134217727,
     15510627, 29659223, 134217727, 134217727, 134217727, 134217727, 134217727, 134217330, 134217727, 134217727,
     134217727, 134217727, 134217727, 134217727, 23119932, 134217331, 134217727, 134217727, 134217727, 134217727,
     134217727, 30446169, 134217727, 134217727, 134217727, 134217727, 134217727, 134217727, 19444797, 23906878,
     134217333, 134217727, 134217727, 134217727, 134217727, 24149579, 26799180, 134217309, 134217727, 134217727,
     134217727, 134217727, 27061837, 133995614, 134217727, 134217727, 134217727, 134217727, 134217727, 20758120,
     134217336, 134217727, 134217727, 134217727, 134217727, 134217727, 134017641, 134217727, 134217727, 134217727,
     134217727, 134217727, 134217727, 134018154, 134217727, 134217727, 134217727, 134217727, 134217727, 134217727,
     134018667, 134217727, 134217727, 134217727, 134217727, 134217727, 134217727, 134019180, 134217727, 134217727,
     134217727, 134217727, 134217727, 134217727, 134019693, 134217727, 134217727, 134217727, 134217727, 134217727,
     134217727, 134020206, 134217727, 134217727, 134217727, 134217727, 134217727, 134217727, 134020719, 134217727,
     134217727, 134217727, 134217727, 134217727, 134217727),
    (4194816, 4457504, 8922145, 12648451, 12862995, 13109377, 37767188, 9710256, 13435909, 9972913, 1647156,
     10235570, 6383235, 1949736, 47213188, 38294041, 47452214, 34886682, 11286198, 35132129, 7433783, 59313708,
     7696394, 14755373, 12074169, 59576331, 12336826, 3175049, 16818363, 21330068, 3524673, 49575050, 36471890,
     49814757, 36734560, 21855803, 39067204, 18137792, 60323981, 37260481, 60598466, 51149462, 37530210, 41979588,
     22663230, 51724912, 39641699, 16634566, 52249687, 18919658, 61681778, 42831987, 23382252, 62206665, 53012553,
     23714980, 26555509, 53337691, 19445925, 53600374, 31233702, 24458957, 19975335, 63282296, 24694428, 44164303,
     20233832, 134217424, 134217727, 134217727, 134217727, 134217727, 134217727, 27649705, 54850126, 134217727,
     134217727, 134217727, 134217727, 134217727, 20763818, 134063226, 134217727, 134217727, 134217727, 134217727,
     134217727, 28130036, 134063739, 134217727, 134217727, 134217727, 134217727, 134217727, 28437163, 134064252,
     134217727, 134217727, 134217727, 134217727, 134217727, 28699806, 134064765, 134217727, 134217727, 134217727,
     134217727, 134217727, 28962476, 134065278, 134217727, 134217727, 134217727, 134217727, 134217727, 29225119,
     134065791, 134217727, 134217727, 134217727, 134217727, 134217727, 65363117, 134066351, 134217727, 134217727,
     134217727, 134217727, 134217727, 134066938, 134217727, 134217727, 134217727, 134217727, 134217727, 134217727,
     134217434, 134217727, 134217727, 134217727, 134217727, 134217727, 134217727, 134067963, 134217727, 134217727,
     134217727, 134217727, 134217727, 134217727, 134068476, 134217727, 134217727, 134217727, 134217727, 134217727,
     134217727, 134068989, 134217727, 134217727, 134217727, 134217727, 134217727, 134217727, 134085854, 134217727,
     134217727, 134217727, 134217727, 134217727, 134217727, 134086367, 134217727, 134217727, 134217727, 134217727,
     134217727, 134217727),
    (4194816, 4457504, 4743201, 46138914, 9184817, 5245105, 13198372, 9710208, 33908229, 47205398, 6103046, 13462055,
     10498178, 38104071, 47993369, 34345012, 48256026, 11286148, 48501472, 11548818, 2648762, 11811461, 35223265,
     2907166, 14225084, 49569311, 38541538, 49840208, 17080968, 14515725, 17371875, 38804672, 17605728, 14796993,
     3967114, 25499330, 51153491, 22092005, 15042630, 29410453, 29665989, 51976934, 29928506, 60657294, 52465239,
     30197391, 60847817, 52998294, 23412969, 15832692, 18957034, 16095349, 26291947, 16313434, 42588365, 54039131,
     24195135, 26560207, 24457847, 54647882, 31505572, 40477421, 43361355, 26787567, 43624057, 134217456, 134217727,
     134217727, 134217727, 134217727, 134217727, 134217727, 134217727, 55613543, 32034971, 27610837, 41004109,
     32283754, 44357288, 134217457, 32561367, 28684458, 63502927, 134217727, 134217727, 134217727, 134217727,
     28947101, 57228414, 44891759, 134080219, 134217727, 134217727, 134217727, 64075935, 134217727, 134217727,
     134217727, 134217727, 134217727, 134217727, 64338604, 134217727, 134217727, 134217727, 134217727, 134217727,
     134217727, 45726893, 134217462, 134217727, 134217727, 134217727, 134217727, 134217727, 64839391, 134217727,
     134217727, 134217727, 134217727, 134217727, 134217727, 134217464, 134217727, 134217727, 134217727, 134217727,
     134217727, 134217727, 134217465, 134217727, 134217727, 134217727, 134217727, 134217727, 134217727, 134217466,
     134217727, 134217727, 134217727, 134217727, 134217727, 134217727, 134217467, 134217727, 134217727, 134217727,
     134217727, 134217727, 134217727, 66191101, 134217727, 134217727, 134217727, 134217727, 134217727, 134217727,
     134217727, 134217727, 134217727, 134217727, 134217727, 134217727, 134217727, 134217470, 134217727, 134217727,
     134217727, 134217727, 134217727, 134217727, 134217727, 134217727, 134217727, 134217727, 134217727, 134217727,
     134217727),
    (46137856, 532512, 4473521, 4736178, 46948355, 12854819, 47211524, 47458340, 1321509, 10054707, 1599510,
     10317440, 10579991, 33931288, 48523783, 37761577, 48762934, 34092074, 11368161, 2433563, 7362748, 14485218,
     11893258, 14747677, 7888062, 59512466, 8150719, 3175045, 16818368, 21332614, 35506241, 50885645, 38569042,
     51167246, 15536195, 51422949, 4002372, 18188897, 15804646, 36211910, 52209762, 36556359, 52472381, 36731976,
     39162467, 52997352, 36994672, 29659851, 26287337, 61446231, 29989464, 54078699, 61924938, 23382671, 42064591,
     62449872, 23645345, 30777931, 23932655, 20006098, 63022710, 134217727, 134217727, 134217727, 134217727,
     134217727, 134217727, 134217727, 134217727, 134217727, 134217727, 134217727, 134217727, 55621784, 134217457,
     134217727, 134217727, 134217727, 134217727, 134217727, 24432291, 55897677, 134079652, 134217727, 134217727,
     134217727, 134217727, 20495464, 24988374, 40169551, 56423017, 134217459, 134217727, 134217727, 32035994,
     28134616, 134080635, 134217727, 134217727, 134217727, 134217727, 28397273, 40744060, 64289389, 134217727,
     134217727, 134217727, 134217727, 28922075, 64600190, 134217727, 134217727, 134217727, 134217727, 134217727,
     33349276, 134082269, 134217727, 134217727, 134217727, 134217727, 134217727, 44678313, 134217464, 134217727,
     134217727, 134217727, 134217727, 134217727, 44907231, 134217465, 134217727, 134217727, 134217727, 134217727,
     134217727, 134083742, 134217727, 134217727, 134217727, 134217727, 134217727, 134217727, 65879724, 134217727,
     134217727, 134217727, 134217727, 134217727, 134217727, 134084781, 134217727, 134217727, 134217727, 134217727,
     134217727, 134217727, 134085294, 134217727, 134217727, 134217727, 134217727, 134217727, 134217727, 134085807,
     134217727, 134217727, 134217727, 134217727, 134217727, 134217727, 134217471, 134217727, 134217727, 134217727,
     134217727, 134217727, 134217727),
    (4194816, 4457504, 8922145, 58744835, 1066515, 9447473, 9710130, 59072517, 59264022, 10235398, 46465075, 1855512,
     46727907, 2118169, 59790362, 7169588, 60035627, 11548802, 47191093, 60316189, 7931573, 37754414, 12336871,
     47716406, 16818308, 17081064, 34871953, 48006240, 14425321, 48268882, 25547910, 48504388, 21832939, 35418181,
     61961286, 35694690, 38656699, 22311561, 62486599, 25982064, 62723158, 29659223, 29983424, 36561085, 30191716,
     23454398, 36730559, 63498313, 15766618, 26576020, 63760987, 16029325, 19970190, 51218550, 26863678, 54599261,
     31234805, 134037567, 134217727, 134217727, 134217727, 134217727, 134217727, 134217727, 134217727, 134217727,
     134217727, 134217727, 134217727, 134217727, 134217727, 134217727, 134217727, 24694421, 42331214, 134217425,
     134217727, 134217727, 134217727, 134217727, 20758120, 51768952, 31773382, 55133432, 134217727, 134217727,
     134217727, 65336426, 134063779, 134217727, 134217727, 134217727, 134217727, 134217727, 65599083, 28414116,
     43382396, 134217428, 134217727, 134217727, 134217727, 66124397, 134064839, 134217727, 134217727, 134217727,
     134217727, 134217727, 66387054, 29207718, 53038846, 134032639, 134217727, 134217727, 134217727, 52756183,
     56709324, 134033065, 134217727, 134217727, 134217727, 134217727, 44675787, 57514714, 45194411, 134033628,
     134217727, 134217727, 134217727, 58284765, 134034127, 134217727, 134217727, 134217727, 134217727, 134217727,
     45989550, 134034587, 134217727, 134217727, 134217727, 134217727, 134217727, 134217727, 134217727, 134217727,
     134217727, 134217727, 134217727, 134217727, 134035613, 134217727, 134217727, 134217727, 134217727, 134217727,
     134217727, 134217727, 134217727, 134217727, 134217727, 134217727, 134217727, 134217727, 134036639, 134217727,
     134217727, 134217727, 134217727, 134217727, 134217727, 134217727, 134217727, 134217727, 134217727, 134217727,
     134217727, 134217727),
    (8389120, 8651792, 4736017, 9199619, 1073683, 13117476, 33565221, 13484037, 33827878, 6049286, 10575924,
     58986008, 34091561, 2212917, 46412842, 11388470, 34345499, 11625616, 59773980, 34617901, 60059315, 2898990,
     12349585, 34957343, 16818188, 17081062, 3500678, 21525223, 35482690, 25173138, 15323203, 3967059, 25547447,
     15536197, 18444435, 22140041, 25784892, 50452053, 61936711, 29404221, 36533441, 62186083, 50900542, 23140540,
     49079368, 30179054, 26286787, 62728281, 30446222, 37609661, 51440218, 23906976, 42306289, 30970972, 42543806,
     63499851, 24463046, 43093747, 31496294, 27085503, 43592798, 24957172, 43880525, 31759465, 44143349, 32022122,
     28175562, 64853627, 32561321, 44691607, 53541485, 33086673, 134217424, 134217727, 134217727, 134217727,
     134217727, 134217727, 134217727, 134217727, 33349369, 44954829, 54109848, 54352123, 55139068, 134217727,
     134217727, 134217727, 134217727, 134217727, 134217727, 134217727, 134217727, 134217727, 40197373, 40459989,
     134064382, 134217727, 134217727, 134217727, 134217727, 134217727, 134217727, 134217727, 134217727, 134217727,
     134217727, 134217727, 56440575, 56210076, 134217727, 134217727, 134217727, 134217727, 134217727, 134217727,
     134217727, 134217727, 134217727, 134217727, 134217727, 134217727, 134066333, 134217727, 134217727, 134217727,
     134217727, 134217727, 134217727, 134217727, 134217727, 134217727, 134217727, 134217727, 134217727, 134217727,
     41793182, 134067421, 134217727, 134217727, 134217727, 134217727, 134217727, 134217727, 134217727, 134217727,
     134217727, 134217727, 134217727, 134217727, 134217436, 134217727, 134217727, 134217727, 134217727, 134217727,
     134217727, 134217727, 134217727, 134217727, 134217727, 134217727, 134217727, 134217727, 134069471, 134217727,
     134217727, 134217727, 134217727, 134217727, 134217727, 134217727, 134217727, 134217727, 134217727, 134217727,
     134217727, 134217727),
    (8389120, 8651792, 8937489, 12846610, 13116963, 5261316, 5524019, 13721605, 1584166, 33566247, 10576437,
     58723864, 6574770, 2163344, 6837302, 7100129, 38015667, 11562626, 2737180, 7625396, 34457144, 2898990, 12413586,
     3262495, 21064761, 15272000, 3441233, 17369829, 3745463, 21545190, 15560771, 3967110, 21807847, 15797829,
     22118585, 16109638, 25766074, 61149296, 29665985, 22614715, 49314930, 22906090, 25984583, 36275827, 51425515,
     30454461, 49883884, 36497992, 26335941, 51965018, 23926975, 62492233, 62729308, 31246989, 24452296, 63017546,
     31505551, 19742922, 134062231, 134217727, 134217727, 134217727, 134217727, 134217727, 134217727, 134217727,
     134217727, 134217727, 134217727, 134217727, 134217727, 134217727, 134217727, 26787489, 63542905, 19975921,
     134062744, 134217727, 134217727, 134217727, 32034978, 134063308, 134217727, 134217727, 134217727, 134217727,
     134217727, 20239011, 43099853, 32283754, 134080206, 134217727, 134217727, 134217727, 54388843, 32561317,
     134217428, 134217727, 134217727, 134217727, 134217727, 28658841, 55900751, 134081178, 134217727, 134217727,
     134217727, 134217727, 56163438, 29183643, 134081663, 134217727, 134217727, 134217727, 134217727, 56447132,
     65092265, 134217463, 134217727, 134217727, 134217727, 134217727, 134066346, 134217727, 134217727, 134217727,
     134217727, 134217727, 134217727, 57012894, 134217727, 134217727, 134217727, 134217727, 134217727, 134217727,
     65623711, 134067451, 134217727, 134217727, 134217727, 134217727, 134217727, 134067884, 134217727, 134217727,
     134217727, 134217727, 134217727, 134217727, 45463805, 134217468, 134217727, 134217727, 134217727, 134217727,
     134217727, 134068910, 134217727, 134217727, 134217727, 134217727, 134217727, 134217727, 66960559, 134085855,
     134217727, 134217727, 134217727, 134217727, 134217727, 134217727, 134217727, 134217727, 134217727, 134217727,
     134217727, 134217727),
    (4194816, 4457504, 8922145, 46161923, 1066515, 9447473, 1329685, 46425312, 46681110, 10235398, 6406707, 46927400,
     10760930, 6881288, 13723690, 11286243, 37841417, 11548801, 59774005, 47733277, 7931109, 38016558, 14179871,
     60299447, 48267344, 17080963, 60583437, 48530514, 60824708, 38307424, 3967059, 14775429, 61114977, 18425531,
     35156714, 18655330, 18918076, 49614528, 15324771, 50651222, 19234028, 62197873, 22857787, 50139842, 62448728,
     19498556, 16066675, 62698085, 30479422, 51412619, 19706982, 51765365, 39182939, 54586444, 63486092, 27102417,
     31234653, 52274317, 39429875, 20495464, 37589204, 31497823, 64036053, 56160873, 134037705, 134217727, 134217727,
     134217727, 134217727, 134217727, 134217727, 134217727, 134217727, 53015658, 32298741, 56487115, 39647340,
     28684535, 134038141, 134217727, 134217378, 134217727, 134217727, 134217727, 134217727, 134217727, 134217727,
     33086681, 57274572, 53804655, 39958265, 42842276, 134217727, 134217727, 134217727, 134217727, 134217727,
     134217727, 134217727, 134217727, 134217727, 54115066, 54377723, 43368188, 134217727, 134217727, 134217727,
     134217727, 134217382, 134217727, 134217727, 134217727, 134217727, 134217727, 134217727, 40499865, 66926334,
     134217383, 134217727, 134217727, 134217727, 134217727, 134217384, 134217727, 134217727, 134217727, 134217727,
     134217727, 134217727, 41243804, 134217385, 134217727, 134217727, 134217727, 134217727, 134217727, 134217727,
     134217727, 134217727, 134217727, 134217727, 134217727, 134217727, 44907692, 134217727, 134217727, 134217727,
     134217727, 134217727, 134217727, 134217727, 134217727, 134217727, 134217727, 134217727, 134217727, 134217727,
     45440159, 134217727, 134217727, 134217727, 134217727, 134217727, 134217727, 134217727, 134217727, 134217727,
     134217727, 134217727, 134217727, 134217727, 134217391, 134217727, 134217727, 134217727, 134217727, 134217727,
     134217727),
)
NF = F // NC
ROWS = ('E3', 'E1', 'P0', 'P1', 'E2', 'P3', 'P2')
ITEMS = ('own', *ROWS, *sorted(NAMES.values()))
PIECE = {n: p for p, n in NAMES.items()}


def whiten(spectra, quality, put):
    here = lax.broadcasted_iota(jnp.int32, (CH, CH), 0) == lax.broadcasted_iota(jnp.int32, (CH, CH), 1)
    usable = jnp.sum(jnp.where(here, quality[...].astype(jnp.float32), 0.0), axis=1, keepdims=True)

    def parts(f):
        values = spectra[f].astype(jnp.float32)
        real_part, imag_part = values[:, :W], values[:, W:]
        return real_part, imag_part, real_part * real_part + imag_part * imag_part

    def add(f, total):
        return total + parts(f)[2]

    mean_energy = lax.fori_loop(0, F, add, jnp.zeros((CH, W), jnp.float32)) / F

    def scale(f, carry):
        real_part, imag_part, energy = parts(f)
        factor = usable / jnp.sqrt(energy + mean_energy + 1e-06)
        put(f, jnp.concatenate([real_part * factor, imag_part * factor], axis=1).astype(jnp.bfloat16))
        return carry

    lax.fori_loop(0, F, scale, 0)


def any_of(q, places):
    hit = q < 0
    for place in places:
        hit = hit | (q == place)
    return hit


def gather_kernel(spectra, quality, cross, rowb, colb, steps, local_sem, row_sem, col_sem, sib_sem, srow_sem, sr_sem,
                  scol_sem, ssib_sem):
    row, col = lax.axis_index("row"), lax.axis_index("col")
    core, x, y_lo = row % 2, (row // 2) % 4, row // 8
    z, y_hi = col // 2, col % 2
    y = y_hi * 2 + y_lo

    def at(xx, yy, zz, cc):
        return {"row": (yy % 2) * 8 + xx * 2 + cc, "col": zz * 2 + yy // 2}

    x_up, x_dn = at((x + 1) % 4, y, z, core), at((x + 3) % 4, y, z, core)
    z_up, z_dn = at(x, y, (z + 1) % 4, core), at(x, y, (z + 3) % 4, core)
    sibling = at(x, y, z, 1 - core)
    partner = at(x, (y + 2) % 4, z, core)
    pair = at(x, y_hi * 2 + 1 - y_lo, z, core)
    other = at(x, (y + 3 + 2 * y_lo) % 4, z, core)

    q = (x + 4 - col % 4) % 4
    mirror = (y_lo + 2 - col // 4) % 2
    place = mirror * 4 + q
    k = y_lo * 4 + x
    is_root = k == col
    not_root = jnp.logical_not(is_root)
    feeds = (z == k // 2) & (y_hi != k % 2)

    def ident(piece):
        half = y_hi if piece[0] == 'E' else 1 - y_hi
        return ((z + int(piece[1])) % 4) * 2 + half

    ids = {p: ident(p) for p in NAMES}

    def chunk(g):
        return pl.ds(g * NF, NF)

    def remote(src, dst, send, recv, to):
        pltpu.make_async_remote_copy(src, dst, send, recv, device_id=to, device_id_type=MESH).start()

    def row_send(slot, piece, g, to):
        part = rowb.at[ids[piece], chunk(g)]
        remote(part, part, srow_sem.at[slot], row_sem.at[ids[piece], g], to)

    def col_send(src, slot, way, piece, g, to):
        dst = colb.at[core * 8 + ids[piece], chunk(g)]
        remote(dst if src is None else src, dst, scol_sem.at[slot, way], col_sem.at[ids[piece], g], to)

    def done(ref, sem):
        pltpu.make_async_copy(ref, ref, sem).wait()

    slots = {n: i for i, n in enumerate(PIECE)}
    barrier = pltpu.get_barrier_semaphore()
    for peer in (x_up, x_dn, pair, other, z_up, z_dn, sibling, partner):
        pl.semaphore_signal(barrier, inc=1, device_id=peer, device_id_type=MESH)

    def put(f, values):
        rowb[ids['E0'], f] = values

    whiten(spectra, quality, put)
    for i in range(len(ORDER[0])):
        word = jnp.int32(ORDER[0][i])
        for p in range(1, 8):
            word = jnp.where(place == p, ORDER[p][i], word)
        steps[i] = word
    pl.semaphore_wait(barrier, 8)

    def root_step(piece, g):
        name = NAMES[piece]
        src = rowb.at[ids[piece], chunk(g)]
        if name[0] == 'a':
            col_send(src, slots[name], 0, piece, g, x_up)
        if name[0] == 'b':
            col_send(src, slots[name], 1, piece, g, x_dn)

    def first(g, carry):
        row_send(0, 'E0', g, z_up)
        row_send(1, 'E0', g, z_dn)

        @pl.when(is_root)
        def _():
            root_step('E0', g)

        return carry

    lax.fori_loop(0, NC, first, 0)

    def y_own(g):
        row_send(6, 'E0', g, partner)

    feed_slot = {'E' + PIECE[n][1]: i for i, n in enumerate(('y0', 'y1'))}

    def row_step(piece, g):
        done(rowb.at[ids[piece], chunk(g)], row_sem.at[ids[piece], g])
        if piece == 'E3':
            row_send(2, piece, g, z_up)
        if piece == 'P0':
            row_send(3, piece, g, z_up)
            row_send(4, piece, g, z_dn)
        if piece == 'P1':
            row_send(5, piece, g, z_dn)

        @pl.when(is_root)
        def _():
            root_step(piece, g)

        if piece in feed_slot:
            @pl.when(feeds)
            def _():
                dst = colb.at[core * 8 + ids[piece], chunk(g)]
                remote(rowb.at[ids[piece], chunk(g)], dst, sr_sem.at[feed_slot[piece]], col_sem.at[ids[piece], g], other)

    on_root_row = mirror == 0
    ways = {}
    for name in slots:
        up = on_root_row & any_of(q, (1, 2)) & (name[0] == 'a')
        down = on_root_row & any_of(q, (3, 2)) & (name[0] == 'b')
        over = jnp.where(on_root_row, any_of(q, [p for p in (1, 2, 3) if name in ENTRY[p]]),
                         any_of(q, (1, 2, 3)) & (name[0] == 'y'))
        enters = [p for p in range(4) if name in ENTRY[p]][0]
        order = ENTRY[enters].index(name)
        mirrored = mirror == 1
        full = mirrored & (q == enters)
        up_half = mirrored & (q == (enters + 1) % 4)
        down_half = mirrored & (q == (enters + 3) % 4)
        ways[name] = (up | full, up_half, down | full, down_half, over, order)

    def col_step(name, g):
        piece = PIECE[name]
        slot = slots[name]
        done(colb.at[core * 8 + ids[piece], chunk(g)], col_sem.at[ids[piece], g])
        up, up_half, down, down_half, over, order = ways[name]

        @pl.when(up | (up_half & (g % 2 == order)))
        def _():
            col_send(None, slot, 0, piece, g, x_up)

        @pl.when(down | (down_half & (g % 2 != order)))
        def _():
            col_send(None, slot, 1, piece, g, x_dn)

        @pl.when(over)
        def _():
            col_send(None, slot, 2, piece, g, pair)

    my_half = colb.at[pl.ds(core * 8, 8)]

    def swap(g):
        mine = my_half.at[:, chunk(g)]

        @pl.when(is_root)
        def _():
            pltpu.make_async_copy(rowb.at[:, chunk(g)], mine, local_sem.at[g]).start()
            remote(rowb.at[:, chunk(g)], mine, ssib_sem, sib_sem.at[g], sibling)

        @pl.when(not_root)
        def _():
            remote(mine, mine, ssib_sem, sib_sem.at[g], sibling)

    def multiply(g):
        @pl.when(is_root)
        def _():
            done(my_half.at[:, chunk(g)], local_sem.at[g])

        done(my_half.at[:, chunk(g)], sib_sem.at[g])

        def two_bins(h, carry):
            parts = []
            for e in range(2):
                f = g * NF + h * 2 + e
                lhs = rowb[:, f].reshape(8 * CH, 2 * W)
                turned = jnp.concatenate([lhs[:, W:], -lhs[:, :W]], axis=1)
                rhs = colb[:, f].reshape(16 * CH, 2 * W)
                parts.append(lax.dot_general(jnp.concatenate([lhs, turned], axis=0), rhs, (((1,), (1,)), ((), ())),
                                             preferred_element_type=jnp.float32))
            for c in range(2):
                both = [p[c * 256:(c + 1) * 256].reshape(32, 8, 512) for p in parts]
                cross[c, :, g * (NF // 2) + h] = jnp.concatenate(both, axis=1).astype(jnp.bfloat16)
            return carry

        lax.fori_loop(0, NF // 2, two_bins, 0)

    acts = [functools.partial(row_step, n) if n in ROWS else functools.partial(col_step, n) if n in PIECE
            else y_own for n in ITEMS]

    def choose(item, g, low, high):
        if high - low == 1:
            acts[low](g)
            return
        middle = (low + high) // 2

        @pl.when(item < middle)
        def _():
            choose(item, g, low, middle)

        @pl.when(item >= middle)
        def _():
            choose(item, g, middle, high)

    def three(i, carry):
        def one(_, word):
            step = lax.rem(word, 512)
            item, g = lax.div(step, 16), lax.rem(step, 16)

            @pl.when(item < len(ITEMS))
            def _():
                choose(item, g, 0, len(ITEMS))

            return lax.div(word, 512)

        lax.fori_loop(0, 3, one, steps[i])
        return carry

    lax.fori_loop(0, BEFORE, three, 0)

    swap(0)

    def with_multiply(g, carry):
        start = BEFORE + g * BETWEEN
        lax.fori_loop(start, start + BETWEEN, three, 0)
        swap(g + 1)
        multiply(g)
        return carry

    lax.fori_loop(0, NC - 1, with_multiply, 0)
    multiply(NC - 1)

    whole = rowb.at[0]
    half_piece = rowb.at[0, pl.ds(0, F // 2)]
    for i in range(7):
        done(whole, srow_sem.at[i])

    @pl.when(feeds)
    def _():
        done(whole, sr_sem.at[0])
        done(whole, sr_sem.at[1])

    for name in slots:
        up, up_half, down, down_half, over, _ = ways[name]
        slot = slots[name]
        for way, full, part, letter in ((0, up, up_half, 'a'), (1, down, down_half, 'b')):
            @pl.when(jnp.where(is_root, name[0] == letter, full))
            def _(slot=slot, way=way):
                done(whole, scol_sem.at[slot, way])

            @pl.when(not_root & part)
            def _(slot=slot, way=way):
                done(half_piece, scol_sem.at[slot, way])

        @pl.when(not_root & over)
        def _(slot=slot):
            done(whole, scol_sem.at[slot, 2])


    done(my_half, ssib_sem)


def gather_cross(spectra, quality):
    piece = (F, CH, 2 * W)
    vmem = pl.BlockSpec(memory_space=pltpu.VMEM)
    return pl.pallas_call(
        gather_kernel,
        out_shape=pltpu.VMEM((2, 32, F // 2, 16, 512), jnp.bfloat16),
        in_specs=[vmem, vmem],
        out_specs=vmem,
        scratch_shapes=[
            pltpu.VMEM((8, *piece), jnp.bfloat16),
            pltpu.VMEM((16, *piece), jnp.bfloat16),
            pltpu.SMEM((len(ORDER[0]),), jnp.int32),
            pltpu.SemaphoreType.DMA((NC,)),
            pltpu.SemaphoreType.DMA((8, NC)),
            pltpu.SemaphoreType.DMA((8, NC)),
            pltpu.SemaphoreType.DMA((NC,)),
            pltpu.SemaphoreType.DMA((7,)),
            pltpu.SemaphoreType.DMA((2,)),
            pltpu.SemaphoreType.DMA((8, 3)),
            pltpu.SemaphoreType.DMA,
        ],
        compiler_params=pltpu.CompilerParams(collective_id=0, has_side_effects=True, vmem_limit_bytes=40 << 20),
        name="gather_cross",
    )(spectra, quality.reshape(1, CH))


def lag_matrices():
    lag = np.arange(HALF + 1, dtype=np.float32)
    frequency = np.arange(F, dtype=np.float32) + np.float32(1.0)
    angles = np.float32(2.0 * math.pi) * frequency[None, :] * lag[:, None] / np.float32(2.0 * LAGS)
    eye = np.eye(8, dtype=np.float32)
    return [np.kron(m, eye).astype(jnp.bfloat16) for m in (np.cos(angles), -np.sin(angles))]


def lag_kernel(mask, cross, even_mat, odd_mat, out, buf, sem):
    rows, cols = out.shape[1], out.shape[2]
    wide = 256
    tile_row = lax.axis_index("row") * (rows // BLK)
    tile_col = lax.axis_index("col") * (cols // BLK)

    def copy(step):
        here = pl.ds(pl.multiple_of(step * 16, 16), 16)
        return pltpu.make_async_copy(buf.at[:, here], out.at[:, here], sem.at[step])

    def one(step, carry):
        here = pl.ds(pl.multiple_of(step * 16, 16), 16)
        for j in range(cols // wide):
            span = slice(j * wide, (j + 1) * wide)
            scale = jnp.concatenate(
                [jnp.full((1, BLK), mask[tile_row + step // 8, tile_col + t].astype(jnp.float32)
                          * (1.0 / math.sqrt(W * F)), jnp.float32)
                 for t in range(j * wide // BLK, (j + 1) * wide // BLK)], axis=1)
            even, odd = [], []
            for h in range(2):
                at = step * 2 + h
                even.append(jnp.dot(even_mat[...], cross[0, at, :, :, span].reshape(F * 8, wide),
                                    preferred_element_type=jnp.float32))
                odd.append(jnp.dot(odd_mat[...], cross[1, at, :, :, span].reshape(F * 8, wide),
                                   preferred_element_type=jnp.float32))
            for m in range(HALF + 1):
                e = [v[m * 8:m * 8 + 8] for v in even]
                o = [v[m * 8:m * 8 + 8] for v in odd]
                if m < HALF:
                    buf[HALF + m, here, span] = (
                        jnp.concatenate([a + b for a, b in zip(e, o)], 0) * scale).astype(out.dtype)
                if m > 0:
                    buf[HALF - m, here, span] = (
                        jnp.concatenate([a - b for a, b in zip(e, o)], 0) * scale).astype(out.dtype)
        copy(step).start()
        return carry

    lax.fori_loop(0, rows // 16, one, 0)

    def finish(step, carry):
        copy(step).wait()
        return carry

    lax.fori_loop(0, rows // 16, finish, 0)


def lag_transform(cross, tile_mask):
    rows, cols = 256, 512
    even_mat, odd_mat = lag_matrices()
    vmem = pl.BlockSpec(memory_space=pltpu.VMEM)
    return pl.pallas_call(
        lag_kernel,
        in_specs=[pl.BlockSpec(memory_space=pltpu.SMEM), vmem, vmem, vmem],
        out_specs=pl.BlockSpec(memory_space=pl.ANY),
        out_shape=jax.ShapeDtypeStruct((LAGS, rows, cols), jnp.bfloat16),
        scratch_shapes=[pltpu.VMEM((LAGS, rows, cols), jnp.bfloat16), pltpu.SemaphoreType.DMA((rows // 16,))],
        compiler_params=pltpu.CompilerParams(vmem_limit_bytes=30 << 20),
        name="lag_transform",
    )(tile_mask, cross, even_mat, odd_mat)


def per_device(spectra, quality, tile_mask):
    cross = gather_cross(spectra, quality)
    return lag_transform(cross, tile_mask)


def solution(mesh):
    placed = (P(None, ("row", "col"), None), P(("row", "col")), P())
    return jax.shard_map(
        per_device, mesh=mesh, in_specs=placed, out_specs=P(None, "row", "col"), check_vma=False
    )
```

```python
import functools
import math

import jax
import jax.numpy as jnp
import numpy as np
from jax import lax
from jax.experimental import pallas as pl
from jax.experimental.pallas import tpu as pltpu
from jax.sharding import PartitionSpec as P

F = 32
LAGS = 64
HALF = LAGS // 2
W = 256
BLK = 128
CH = 32
MESH = pl.DeviceIdType.MESH

NAMES = {'E0': 'a0', 'E3': 'a1', 'E2': 'a2', 'E1': 'b0', 'P0': 'b1', 'P1': 'b2', 'P2': 'y0', 'P3': 'y1'}
ENTRY = {0: ('y0', 'y1'), 1: ('a0', 'a2'), 2: ('a1', 'b1'), 3: ('b2', 'b0')}
NC = 16
BEFORE, BETWEEN = 68, 7
ORDER = (
    (8389120, 4473360, 8937474, 811538, 9446947, 9701396, 9987093, 10226198, 10511895, 10751000, 11013657, 11298842,
     11538459, 7625244, 12063285, 8150558, 16818186, 21239350, 17350721, 21502007, 17875523, 18130445, 3705912,
     18655330, 134217328, 134217727, 134217727, 134217727, 134217727, 134217727, 134217727, 134217727, 134217727,
     134217727, 134217727, 134217727, 134217727, 134217727, 134217727, 134217727, 134217727, 134217727, 134217727,
     134217727, 134217727, 134217727, 134217727, 134217727, 134217727, 134217727, 134217727, 134217727, 134217727,
     134217727, 134217727, 134217727, 134217727, 134217727, 134217727, 134217727, 134217727, 134217727, 134217727,
     134217727, 134217727, 134217727, 134217727, 134217727, 22311439, 29666403, 134217727, 134217727, 134217727,
     134217727, 134217727, 134014024, 134217727, 134217727, 134217727, 134217727, 134217727, 134217727, 30191162,
     134217727, 134217727, 134217727, 134217727, 134217727, 134217727, 15511652, 30454345, 134217727, 134217727,
     134217727, 134217727, 134217727, 15774837, 133993573, 134217727, 134217727, 134217727, 134217727, 134217727,
     30964315, 24149067, 19970662, 134217727, 134217727, 134217727, 134217727, 16554615, 20500062, 134217727,
     134217727, 134217727, 134217727, 134217727, 27324511, 134217295, 134217727, 134217727, 134217727, 134217727,
     134217727, 134017641, 134217727, 134217727, 134217727, 134217727, 134217727, 134217727, 134018154, 134217727,
     134217727, 134217727, 134217727, 134217727, 134217727, 134018667, 134217727, 134217727, 134217727, 134217727,
     134217727, 134217727, 134019180, 134217727, 134217727, 134217727, 134217727, 134217727, 134217727, 134019693,
     134217727, 134217727, 134217727, 134217727, 134217727, 134217727, 33087086, 134217727, 134217727, 134217727,
     134217727, 134217727, 134217727, 134217343, 134217727, 134217727, 134217727, 134217727, 134217727, 134217727),
    (33554944, 33832976, 541201, 4785200, 811554, 9184899, 5310514, 34867236, 13388309, 9972870, 6098437, 13721639,
     6361328, 46402600, 10760841, 1958592, 11023498, 36529205, 50615835, 36704498, 14178332, 7674547, 47190573,
     37348919, 37510174, 2645535, 37873845, 50888784, 38016568, 47743569, 17376501, 21545143, 15068172, 51152531,
     17901665, 15298573, 39102199, 25784901, 3706006, 48789240, 18689620, 22382607, 15786136, 65352379, 18918499,
     49362033, 16070394, 22857917, 65856585, 23169692, 49866397, 41464382, 50198644, 16596581, 54585930, 41989373,
     42251974, 30971646, 42514641, 26846463, 134070435, 134217727, 134217727, 134217727, 134217727, 134217727,
     134217727, 134217727, 24440396, 59084452, 134217727, 134217727, 134217727, 134217727, 134217727, 27109029,
     31496798, 134071462, 134217727, 134217727, 134217727, 134217727, 43826900, 134217443, 134217727, 134217727,
     134217727, 134217727, 134217727, 31759573, 52514920, 56185449, 59831375, 134217727, 134217727, 134217727,
     56448106, 32331371, 134073033, 134217727, 134217727, 134217727, 134217727, 32594028, 45406936, 60396669,
     134217727, 134217727, 134217727, 134217727, 33119342, 134074073, 134217727, 134217727, 134217727, 134217727,
     134217727, 33381999, 134074571, 134217727, 134217727, 134217727, 134217727, 134217727, 134075098, 134217727,
     134217727, 134217727, 134217727, 134217727, 134217727, 134075596, 134217727, 134217727, 134217727, 134217727,
     134217727, 134217727, 57530061, 134217727, 134217727, 134217727, 134217727, 134217727, 134217727, 134076636,
     134217727, 134217727, 134217727, 134217727, 134217727, 134217727, 58055374, 134217727, 134217727, 134217727,
     134217727, 134217727, 134217727, 58302190, 134217727, 134217727, 134217727, 134217727, 134217727, 134217727,
     134078175, 134217727, 134217727, 134217727, 134217727, 134217727, 134217727),
    (4194816, 8659488, 4743170, 33579554, 9184771, 9447553, 1074306, 9710256, 5857923, 1378342, 6127667, 46729767,
     1593368, 6652550, 35416105, 6819507, 35774506, 11286196, 2167349, 47470620, 7673073, 2458669, 12074123,
     63466678, 12336780, 36967607, 51150928, 2911987, 37257809, 37520568, 25290937, 17569874, 48832568, 17875701,
     3508369, 38308435, 15068347, 49340500, 22289555, 18446996, 25697905, 39089399, 29928645, 65109142, 39614039,
     18710131, 23119512, 54556788, 23409401, 40471669, 23721021, 31012561, 18925630, 31323858, 16561820, 52247292,
     66359900, 24487582, 55656056, 19446885, 55967392, 66667129, 19709640, 134070434, 134217727, 134217727,
     134217727, 134217727, 32034006, 27111075, 52774988, 43316840, 59298520, 53038157, 59045994, 134217727,
     134217727, 134217727, 134217727, 134217727, 134217727, 134217727, 28153511, 44080253, 44357849, 28638412,
     59618474, 134217727, 134217727, 33332846, 59873963, 134217727, 134217727, 134217727, 134217727, 134217727,
     57497711, 134217445, 134217727, 134217727, 134217727, 134217727, 134217727, 45718701, 134073564, 134217727,
     134217727, 134217727, 134217727, 134217727, 54353629, 134217447, 134217727, 134217727, 134217727, 134217727,
     134217727, 60931806, 134217727, 134217727, 134217727, 134217727, 134217727, 134217727, 134217449, 134217727,
     134217727, 134217727, 134217727, 134217727, 134217727, 134075627, 134217727, 134217727, 134217727, 134217727,
     134217727, 134217727, 134217727, 134217727, 134217727, 134217727, 134217727, 134217727, 134217727, 134217452,
     134217727, 134217727, 134217727, 134217727, 134217727, 134217727, 134217453, 134217727, 134217727, 134217727,
     134217727, 134217727, 134217727, 134217454, 134217727, 134217727, 134217727, 134217727, 134217727, 134217727,
     134217455, 134217727, 134217727, 134217727, 134217727, 134217727, 134217727),
    (8389120, 4473360, 8937474, 46162450, 4998659, 9462961, 33652756, 5523972, 33907763, 50605094, 13698053,
     46935591, 10608771, 47189016, 6574724, 63269429, 11013765, 35226650, 47724075, 11538674, 48000028, 7625351,
     2459191, 12183176, 36007966, 63979055, 36270602, 14712912, 36443834, 51413585, 36825657, 25261634, 36968530,
     49409091, 15239265, 3504782, 64784979, 3771023, 18393278, 37875771, 50126946, 4006485, 38400720, 15786567,
     25996486, 38566514, 65580753, 30254228, 39091272, 30453959, 55389435, 39629412, 23625428, 66120265, 31011029,
     40210685, 66622555, 26555606, 66907740, 24458967, 19775689, 56703096, 41209057, 52992094, 27081849, 53331039,
     56966733, 134037731, 53517416, 134217377, 134217727, 134217727, 134217727, 134217727, 134217727, 32093289,
     42584143, 134217727, 134217727, 134217727, 134217727, 134217727, 60136042, 134217379, 134217727, 134217727,
     134217727, 134217727, 134217727, 57472619, 134217380, 134217727, 134217727, 134217727, 134217727, 134217727,
     54065260, 134217381, 134217727, 134217727, 134217727, 134217727, 134217727, 57735789, 33086694, 134217382,
     134217727, 134217727, 134217727, 134217727, 33349341, 134041319, 134217727, 134217727, 134217727, 134217727,
     134217727, 44159183, 134217727, 134217727, 134217727, 134217727, 134217727, 134217727, 58544862, 134217449,
     134217727, 134217727, 134217727, 134217727, 134217727, 134075562, 134217727, 134217727, 134217727, 134217727,
     134217727, 134217727, 134076075, 134217727, 134217727, 134217727, 134217727, 134217727, 134217727, 134076588,
     134217727, 134217727, 134217727, 134217727, 134217727, 134217727, 62217389, 134217727, 134217727, 134217727,
     134217727, 134217727, 134217727, 134077615, 134217727, 134217727, 134217727, 134217727, 134217727, 134217727,
     134217455, 134217727, 134217727, 134217727, 134217727, 134217727, 134217727),
    (4194816, 8659488, 8922114, 811568, 62932499, 63195156, 9710084, 5832754, 1434662, 10235521, 6416048, 13372456,
     10760834, 1960113, 13653018, 11286147, 34728626, 11548680, 11811574, 34869939, 12074231, 47284277, 2645535,
     50662648, 35422288, 2976505, 14189137, 17350792, 65542326, 35948114, 17875707, 14424759, 36211283, 48270588,
     22070286, 14809794, 36495431, 66592441, 26024021, 29666490, 51248781, 29913672, 58793047, 26310259, 59019864,
     30454415, 38084666, 30767330, 15563354, 23893093, 38389366, 15825995, 59844188, 19970662, 31293124, 60062285,
     41991376, 134217727, 134217727, 134217727, 134217727, 134217727, 134217727, 134217727, 134217727, 134217727,
     134217727, 134217727, 38837351, 24935654, 54849685, 134038079, 134217727, 134217727, 134217727, 20762855,
     134038738, 134217727, 134217727, 134217727, 134217727, 134217727, 51704425, 27870952, 134063738, 134217727,
     134217727, 134217727, 134217727, 28126953, 61418619, 32561316, 134217428, 134217727, 134217727, 134217727,
     28658411, 134064765, 134217727, 134217727, 134217727, 134217727, 134217727, 28914412, 33151640, 56155814,
     134057198, 134217727, 134217727, 134217727, 43900631, 44105432, 56971930, 44676251, 57497244, 134057644,
     134217727, 41269421, 41508061, 41794735, 134058207, 134217727, 134217727, 134217727, 134217417, 134217727,
     134217727, 134217727, 134217727, 134217727, 134217727, 134217418, 134217727, 134217727, 134217727, 134217727,
     134217727, 134217727, 134217419, 134217727, 134217727, 134217727, 134217727, 134217727, 134217727, 134217420,
     134217727, 134217727, 134217727, 134217727, 134217727, 134217727, 134217421, 134217727, 134217727, 134217727,
     134217727, 134217727, 134217727, 134217422, 134217727, 134217727, 134217727, 134217727, 134217727, 134217727,
     134217423, 134217727, 134217727, 134217727, 134217727, 134217727, 134217727),
    (8389120, 4473360, 4736002, 811568, 33564195, 33826852, 5523972, 10084402, 1377302, 6049521, 10552883, 63441944,
     34615849, 11013808, 13755930, 34879019, 50335921, 35141676, 7625460, 64324105, 12127797, 64578590, 2637359,
     21063304, 64777280, 17080843, 65104009, 21545026, 50926604, 14545475, 47482977, 47717003, 65571411, 25790092,
     3798598, 18655288, 4004535, 66117717, 37821497, 18918499, 37616241, 15299256, 19181156, 38141042, 15829051,
     66905688, 23362234, 38387828, 19430501, 38631029, 49315418, 31048283, 24193099, 49597666, 31277205, 51690060,
     39437985, 24694434, 59830349, 24987326, 43069119, 27325006, 43331813, 134062185, 134217727, 134217727,
     134217727, 134217727, 20794566, 60347514, 28135065, 60634235, 32561320, 134217425, 134217727, 134217426,
     134217727, 134217727, 134217727, 134217727, 134217727, 134217727, 32823977, 44683419, 40959086, 29185769,
     134063743, 134217727, 134217727, 52254954, 134217428, 134217727, 134217727, 134217727, 134217727, 134217727,
     61684397, 61947054, 134064815, 134217727, 134217727, 134217727, 134217727, 56180461, 134217727, 134217727,
     134217727, 134217727, 134217727, 134217727, 52813000, 134065903, 134217727, 134217727, 134217727, 134217727,
     134217727, 134217432, 134217727, 134217727, 134217727, 134217727, 134217727, 134217727, 53327050, 134217433,
     134217727, 134217727, 134217727, 134217727, 134217727, 134217727, 134217727, 134217727, 134217727, 134217727,
     134217727, 134217727, 53844188, 134217435, 134217727, 134217727, 134217727, 134217727, 134217727, 134217727,
     134217727, 134217727, 134217727, 134217727, 134217727, 134217727, 54369502, 134217437, 134217727, 134217727,
     134217727, 134217727, 134217727, 134217727, 134217727, 134217727, 134217727, 134217727, 134217727, 134217727,
     134217439, 134217727, 134217727, 134217727, 134217727, 134217727, 134217727),
    (8389120, 4473360, 8937474, 811538, 13116963, 1058852, 5524019, 5786752, 13697541, 46149159, 62926888, 10814470,
     50422297, 1862385, 34354218, 7100146, 2164929, 11625526, 11920924, 14509597, 12126729, 35252254, 47201839,
     21096970, 47476800, 35395266, 17080889, 17371382, 21545142, 17690124, 25498307, 15298116, 18130445, 22091000,
     3764336, 22409787, 29658256, 4003513, 65566818, 22616209, 51475570, 16035579, 66132595, 26027079, 37283928,
     66418238, 38595161, 49329295, 26274964, 66616904, 39190135, 51739227, 49844828, 39383133, 26554080, 50107486,
     59060345, 40146527, 134037712, 134217727, 134217727, 134217727, 134217727, 134217727, 134217727, 134217727,
     134217727, 134217727, 51967078, 27116753, 55129164, 134217377, 134217727, 134217727, 134217727, 40695400,
     134038755, 134217727, 134217727, 134217727, 134217727, 134217727, 20265065, 134039251, 134217727, 134217727,
     134217727, 134217727, 134217727, 52230250, 28166356, 20527741, 134039765, 134217727, 134217727, 134217727,
     56179820, 28638373, 134072991, 134217727, 134217727, 134217727, 134217727, 20765862, 56426184, 52747943,
     134073560, 134217727, 134217727, 134217727, 44151498, 134074059, 134217727, 134217727, 134217727, 134217727,
     134217727, 57252009, 57514666, 134217448, 134217727, 134217727, 134217727, 134217727, 134075086, 134217727,
     134217727, 134217727, 134217727, 134217727, 134217727, 45201579, 61462223, 134217727, 134217727, 134217727,
     134217727, 134217727, 134217727, 134217727, 134217727, 134217727, 134217727, 134217727, 134217727, 58284765,
     45996718, 134076639, 134217727, 134217727, 134217727, 134217727, 134217727, 134217727, 134217727, 134217727,
     134217727, 134217727, 134217727, 134077679, 134217727, 134217727, 134217727, 134217727, 134217727, 134217727,
     134217727, 134217727, 134217727, 134217727, 134217727, 134217727, 134217727),
    (4194816, 8659488, 8922114, 811568, 13125139, 1067028, 9710256, 9972976, 46402099, 10235633, 6357044, 63441960,
     10760882, 1862273, 63722522, 7144627, 2222123, 11548864, 34368692, 2382365, 64318145, 14441502, 8252548,
     47715375, 16818309, 21239543, 48001089, 17428614, 21545017, 17662988, 25522425, 3477060, 18130568, 15299322,
     3740355, 48794708, 65855586, 36206165, 49149967, 15786567, 37878358, 22864995, 30242955, 49675409, 36745288,
     30440077, 51425892, 49839359, 30708314, 31047826, 37584526, 19474011, 54641215, 31242341, 54903956, 19737181,
     59614328, 55364805, 39360606, 59877497, 39632487, 39955021, 27372773, 56462414, 32099433, 56701519, 134037610,
     134217727, 28160666, 42323579, 134217727, 134217727, 134217727, 134217727, 134217727, 60881004, 28685467,
     134038653, 134217727, 134217727, 134217727, 134217727, 33086620, 57511657, 61406831, 134217379, 134217727,
     134217727, 134217727, 134217380, 134217727, 134217727, 134217727, 134217727, 134217727, 134217727, 61684444,
     61979294, 62241951, 134217381, 134217727, 134217727, 134217727, 134040799, 134217727, 134217727, 134217727,
     134217727, 134217727, 134217727, 52813000, 44143855, 134217383, 134217727, 134217727, 134217727, 134217727,
     134217727, 134217727, 134217727, 134217727, 134217727, 134217727, 134217727, 53581482, 134042284, 134217727,
     134217727, 134217727, 134217727, 134217727, 134217727, 134217727, 134217727, 134217727, 134217727, 134217727,
     134217727, 54090957, 134217387, 134217727, 134217727, 134217727, 134217727, 134217727, 134217727, 134217727,
     134217727, 134217727, 134217727, 134217727, 134217727, 134044367, 134217727, 134217727, 134217727, 134217727,
     134217727, 134217727, 134217727, 134217727, 134217727, 134217727, 134217727, 134217727, 134217727, 134217391,
     134217727, 134217727, 134217727, 134217727, 134217727, 134217727),
)
NF = F // NC
ROWS = ('E3', 'E1', 'P0', 'P1', 'E2', 'P3', 'P2')
ITEMS = ('own', *ROWS, *sorted(NAMES.values()))
PIECE = {n: p for p, n in NAMES.items()}


def whiten(spectra, quality, put):
    here = lax.broadcasted_iota(jnp.int32, (CH, CH), 0) == lax.broadcasted_iota(jnp.int32, (CH, CH), 1)
    usable = jnp.sum(jnp.where(here, quality[...].astype(jnp.float32), 0.0), axis=1, keepdims=True)

    def parts(f):
        values = spectra[f].astype(jnp.float32)
        real_part, imag_part = values[:, :W], values[:, W:]
        return real_part, imag_part, real_part * real_part + imag_part * imag_part

    def add(f, total):
        return total + parts(f)[2]

    mean_energy = lax.fori_loop(0, F, add, jnp.zeros((CH, W), jnp.float32), unroll=4) / F

    def scale(f, carry):
        real_part, imag_part, energy = parts(f)
        factor = usable / jnp.sqrt(energy + mean_energy + 1e-06)
        put(f, jnp.concatenate([real_part * factor, imag_part * factor], axis=1).astype(jnp.bfloat16))
        return carry

    lax.fori_loop(0, F, scale, 0, unroll=4)


def any_of(q, places):
    hit = q < 0
    for place in places:
        hit = hit | (q == place)
    return hit


def gather_kernel(spectra, quality, cross, rowb, colb, steps, local_sem, row_sem, col_sem, sib_sem, srow_sem, sr_sem,
                  scol_sem, ssib_sem):
    row, col = lax.axis_index("row"), lax.axis_index("col")
    core, x, y_lo = row % 2, (row // 2) % 4, row // 8
    z, y_hi = col // 2, col % 2
    y = y_hi * 2 + y_lo

    def at(xx, yy, zz, cc):
        return {"row": (yy % 2) * 8 + xx * 2 + cc, "col": zz * 2 + yy // 2}

    x_up, x_dn = at((x + 1) % 4, y, z, core), at((x + 3) % 4, y, z, core)
    z_up, z_dn = at(x, y, (z + 1) % 4, core), at(x, y, (z + 3) % 4, core)
    sibling = at(x, y, z, 1 - core)
    partner = at(x, (y + 2) % 4, z, core)
    pair = at(x, y_hi * 2 + 1 - y_lo, z, core)
    other = at(x, (y + 3 + 2 * y_lo) % 4, z, core)

    q = (x + 4 - col % 4) % 4
    mirror = (y_lo + 2 - col // 4) % 2
    place = mirror * 4 + q
    k = y_lo * 4 + x
    is_root = k == col
    not_root = jnp.logical_not(is_root)
    feeds = (z == k // 2) & (y_hi != k % 2)

    def ident(piece):
        half = y_hi if piece[0] == 'E' else 1 - y_hi
        return ((z + int(piece[1])) % 4) * 2 + half

    ids = {p: ident(p) for p in NAMES}

    def chunk(g):
        return pl.ds(g * NF, NF)

    def remote(src, dst, send, recv, to):
        pltpu.make_async_remote_copy(src, dst, send, recv, device_id=to, device_id_type=MESH).start()

    def row_send(slot, piece, g, to):
        part = rowb.at[ids[piece], chunk(g)]
        remote(part, part, srow_sem.at[slot], row_sem.at[ids[piece], g], to)

    def col_send(src, slot, way, piece, g, to):
        dst = colb.at[core * 8 + ids[piece], chunk(g)]
        remote(dst if src is None else src, dst, scol_sem.at[slot, way], col_sem.at[ids[piece], g], to)

    def done(ref, sem):
        pltpu.make_async_copy(ref, ref, sem).wait()

    slots = {n: i for i, n in enumerate(PIECE)}
    barrier = pltpu.get_barrier_semaphore()
    for peer in (x_up, x_dn, pair, other, z_up, z_dn, sibling, partner):
        pl.semaphore_signal(barrier, inc=1, device_id=peer, device_id_type=MESH)

    def put(f, values):
        rowb[ids['E0'], f] = values

    whiten(spectra, quality, put)
    for i in range(len(ORDER[0])):
        word = jnp.int32(ORDER[0][i])
        for p in range(1, 8):
            word = jnp.where(place == p, ORDER[p][i], word)
        steps[i] = word
    pl.semaphore_wait(barrier, 8)

    def root_step(piece, g):
        name = NAMES[piece]
        src = rowb.at[ids[piece], chunk(g)]
        if name[0] == 'a':
            col_send(src, slots[name], 0, piece, g, x_up)
        if name[0] == 'b':
            col_send(src, slots[name], 1, piece, g, x_dn)

    def first(g, carry):
        row_send(0, 'E0', g, z_up)
        row_send(1, 'E0', g, z_dn)

        @pl.when(is_root)
        def _():
            root_step('E0', g)

        return carry

    lax.fori_loop(0, NC, first, 0)

    def y_own(g):
        row_send(6, 'E0', g, partner)

    feed_slot = {'E' + PIECE[n][1]: i for i, n in enumerate(('y0', 'y1'))}

    def row_step(piece, g):
        done(rowb.at[ids[piece], chunk(g)], row_sem.at[ids[piece], g])
        if piece == 'E3':
            row_send(2, piece, g, z_up)
        if piece == 'P0':
            row_send(3, piece, g, z_up)
            row_send(4, piece, g, z_dn)
        if piece == 'P1':
            row_send(5, piece, g, z_dn)

        @pl.when(is_root)
        def _():
            root_step(piece, g)

        if piece in feed_slot:
            @pl.when(feeds)
            def _():
                dst = colb.at[core * 8 + ids[piece], chunk(g)]
                remote(rowb.at[ids[piece], chunk(g)], dst, sr_sem.at[feed_slot[piece]], col_sem.at[ids[piece], g], other)

    on_root_row = mirror == 0
    ways = {}
    for name in slots:
        up = on_root_row & any_of(q, (1, 2)) & (name[0] == 'a')
        down = on_root_row & any_of(q, (3, 2)) & (name[0] == 'b')
        over = jnp.where(on_root_row, any_of(q, [p for p in (1, 2, 3) if name in ENTRY[p]]),
                         any_of(q, (1, 2, 3)) & (name[0] == 'y'))
        enters = [p for p in range(4) if name in ENTRY[p]][0]
        order = ENTRY[enters].index(name)
        mirrored = mirror == 1
        full = mirrored & (q == enters)
        up_half = mirrored & (q == (enters + 1) % 4)
        down_half = mirrored & (q == (enters + 3) % 4)
        ways[name] = (up | full, up_half, down | full, down_half, over, order)

    def col_step(name, g):
        piece = PIECE[name]
        slot = slots[name]
        done(colb.at[core * 8 + ids[piece], chunk(g)], col_sem.at[ids[piece], g])
        up, up_half, down, down_half, over, order = ways[name]

        @pl.when(up | (up_half & (g % 2 == order)))
        def _():
            col_send(None, slot, 0, piece, g, x_up)

        @pl.when(down | (down_half & (g % 2 != order)))
        def _():
            col_send(None, slot, 1, piece, g, x_dn)

        @pl.when(over)
        def _():
            col_send(None, slot, 2, piece, g, pair)

    my_half = colb.at[pl.ds(core * 8, 8)]

    def swap(g):
        mine = my_half.at[:, chunk(g)]

        @pl.when(is_root)
        def _():
            pltpu.make_async_copy(rowb.at[:, chunk(g)], mine, local_sem.at[g]).start()
            remote(rowb.at[:, chunk(g)], mine, ssib_sem, sib_sem.at[g], sibling)

        @pl.when(not_root)
        def _():
            remote(mine, mine, ssib_sem, sib_sem.at[g], sibling)

    def multiply(g):
        @pl.when(is_root)
        def _():
            done(my_half.at[:, chunk(g)], local_sem.at[g])

        done(my_half.at[:, chunk(g)], sib_sem.at[g])

        def two_bins(h, carry):
            parts = []
            for e in range(2):
                f = g * NF + h * 2 + e
                lhs = rowb[:, f].reshape(8 * CH, 2 * W)
                turned = jnp.concatenate([lhs[:, W:], -lhs[:, :W]], axis=1)
                rhs = colb[:, f].reshape(16 * CH, 2 * W)
                parts.append(lax.dot_general(jnp.concatenate([lhs, turned], axis=0), rhs, (((1,), (1,)), ((), ())),
                                             preferred_element_type=jnp.float32))
            for c in range(2):
                both = [p[c * 256:(c + 1) * 256].reshape(32, 8, 512) for p in parts]
                cross[c, :, g * (NF // 2) + h] = jnp.concatenate(both, axis=1).astype(jnp.bfloat16)
            return carry

        lax.fori_loop(0, NF // 2, two_bins, 0)

    acts = [functools.partial(row_step, n) if n in ROWS else functools.partial(col_step, n) if n in PIECE
            else y_own for n in ITEMS]

    def choose(item, g, low, high):
        if high - low == 1:
            acts[low](g)
            return
        middle = (low + high) // 2

        @pl.when(item < middle)
        def _():
            choose(item, g, low, middle)

        @pl.when(item >= middle)
        def _():
            choose(item, g, middle, high)

    def three(i, carry):
        def one(_, word):
            step = lax.rem(word, 512)
            item, g = lax.div(step, 16), lax.rem(step, 16)

            @pl.when(item < len(ITEMS))
            def _():
                choose(item, g, 0, len(ITEMS))

            return lax.div(word, 512)

        lax.fori_loop(0, 3, one, steps[i])
        return carry

    lax.fori_loop(0, BEFORE, three, 0)

    swap(0)

    def with_multiply(g, carry):
        start = BEFORE + g * BETWEEN
        lax.fori_loop(start, start + BETWEEN, three, 0)
        swap(g + 1)
        multiply(g)
        return carry

    lax.fori_loop(0, NC - 1, with_multiply, 0)
    multiply(NC - 1)

    whole = rowb.at[0]
    half_piece = rowb.at[0, pl.ds(0, F // 2)]
    for i in range(7):
        done(whole, srow_sem.at[i])

    @pl.when(feeds)
    def _():
        done(whole, sr_sem.at[0])
        done(whole, sr_sem.at[1])

    for name in slots:
        up, up_half, down, down_half, over, _ = ways[name]
        slot = slots[name]
        for way, full, part, letter in ((0, up, up_half, 'a'), (1, down, down_half, 'b')):
            @pl.when(jnp.where(is_root, name[0] == letter, full))
            def _(slot=slot, way=way):
                done(whole, scol_sem.at[slot, way])

            @pl.when(not_root & part)
            def _(slot=slot, way=way):
                done(half_piece, scol_sem.at[slot, way])

        @pl.when(not_root & over)
        def _(slot=slot):
            done(whole, scol_sem.at[slot, 2])


    done(my_half, ssib_sem)


def gather_cross(spectra, quality):
    piece = (F, CH, 2 * W)
    vmem = pl.BlockSpec(memory_space=pltpu.VMEM)
    return pl.pallas_call(
        gather_kernel,
        out_shape=pltpu.VMEM((2, 32, F // 2, 16, 512), jnp.bfloat16),
        in_specs=[vmem, vmem],
        out_specs=vmem,
        scratch_shapes=[
            pltpu.VMEM((8, *piece), jnp.bfloat16),
            pltpu.VMEM((16, *piece), jnp.bfloat16),
            pltpu.SMEM((len(ORDER[0]),), jnp.int32),
            pltpu.SemaphoreType.DMA((NC,)),
            pltpu.SemaphoreType.DMA((8, NC)),
            pltpu.SemaphoreType.DMA((8, NC)),
            pltpu.SemaphoreType.DMA((NC,)),
            pltpu.SemaphoreType.DMA((7,)),
            pltpu.SemaphoreType.DMA((2,)),
            pltpu.SemaphoreType.DMA((8, 3)),
            pltpu.SemaphoreType.DMA,
        ],
        compiler_params=pltpu.CompilerParams(collective_id=0, has_side_effects=True, vmem_limit_bytes=40 << 20),
        name="gather_cross",
    )(spectra, quality.reshape(1, CH))


def lag_matrices():
    lag = np.arange(HALF + 1, dtype=np.float32)
    frequency = np.arange(F, dtype=np.float32) + np.float32(1.0)
    angles = np.float32(2.0 * math.pi) * frequency[None, :] * lag[:, None] / np.float32(2.0 * LAGS)
    eye = np.eye(8, dtype=np.float32)
    return [np.kron(m, eye).astype(jnp.bfloat16) for m in (np.cos(angles), -np.sin(angles))]


def lag_kernel(mask, cross, even_mat, odd_mat, out, buf, sem):
    rows, cols = out.shape[1], out.shape[2]
    wide = 256
    tile_row = lax.axis_index("row") * (rows // BLK)
    tile_col = lax.axis_index("col") * (cols // BLK)

    def copy(step):
        here = pl.ds(pl.multiple_of(step * 16, 16), 16)
        return pltpu.make_async_copy(buf.at[:, here], out.at[:, here], sem.at[step])

    def one(step, carry):
        here = pl.ds(pl.multiple_of(step * 16, 16), 16)
        for j in range(cols // wide):
            span = slice(j * wide, (j + 1) * wide)
            scale = jnp.concatenate(
                [jnp.full((1, BLK), mask[tile_row + step // 8, tile_col + t].astype(jnp.float32)
                          * (1.0 / math.sqrt(W * F)), jnp.float32)
                 for t in range(j * wide // BLK, (j + 1) * wide // BLK)], axis=1)
            even, odd = [], []
            for h in range(2):
                at = step * 2 + h
                even.append(jnp.dot(even_mat[...], cross[0, at, :, :, span].reshape(F * 8, wide),
                                    preferred_element_type=jnp.float32))
                odd.append(jnp.dot(odd_mat[...], cross[1, at, :, :, span].reshape(F * 8, wide),
                                   preferred_element_type=jnp.float32))
            for m in range(HALF + 1):
                e = [v[m * 8:m * 8 + 8] for v in even]
                o = [v[m * 8:m * 8 + 8] for v in odd]
                if m < HALF:
                    buf[HALF + m, here, span] = (
                        jnp.concatenate([a + b for a, b in zip(e, o)], 0) * scale).astype(out.dtype)
                if m > 0:
                    buf[HALF - m, here, span] = (
                        jnp.concatenate([a - b for a, b in zip(e, o)], 0) * scale).astype(out.dtype)
        copy(step).start()
        return carry

    lax.fori_loop(0, rows // 16, one, 0, unroll=4)

    def finish(step, carry):
        copy(step).wait()
        return carry

    lax.fori_loop(0, rows // 16, finish, 0)


def lag_transform(cross, tile_mask):
    rows, cols = 256, 512
    even_mat, odd_mat = lag_matrices()
    vmem = pl.BlockSpec(memory_space=pltpu.VMEM)
    return pl.pallas_call(
        lag_kernel,
        in_specs=[pl.BlockSpec(memory_space=pltpu.SMEM), vmem, vmem, vmem],
        out_specs=pl.BlockSpec(memory_space=pl.ANY),
        out_shape=jax.ShapeDtypeStruct((LAGS, rows, cols), jnp.bfloat16),
        scratch_shapes=[pltpu.VMEM((LAGS, rows, cols), jnp.bfloat16), pltpu.SemaphoreType.DMA((rows // 16,))],
        compiler_params=pltpu.CompilerParams(vmem_limit_bytes=30 << 20),
        name="lag_transform",
    )(tile_mask, cross, even_mat, odd_mat)


def per_device(spectra, quality, tile_mask):
    cross = gather_cross(spectra, quality)
    return lag_transform(cross, tile_mask)


def solution(mesh):
    placed = (P(None, ("row", "col"), None), P(("row", "col")), P())
    return jax.shard_map(
        per_device, mesh=mesh, in_specs=placed, out_specs=P(None, "row", "col"), check_vma=False
    )
```

```python
import functools
import math

import jax
import jax.numpy as jnp
import numpy as np
from jax import lax
from jax.experimental import pallas as pl
from jax.experimental.pallas import tpu as pltpu
from jax.sharding import PartitionSpec as P

F = 32
LAGS = 64
HALF = LAGS // 2
W = 256
BLK = 128
CH = 32
MESH = pl.DeviceIdType.MESH

NAMES = {'E0': 'a0', 'E3': 'a1', 'E2': 'a2', 'E1': 'b0', 'P0': 'b1', 'P1': 'b2', 'P2': 'y0', 'P3': 'y1'}
ENTRY = {0: ('y0', 'y1'), 1: ('a0', 'a2'), 2: ('a1', 'b1'), 3: ('b2', 'b0')}
NC = 16
BEFORE, BETWEEN = 68, 7
ORDER = (
    (8389120, 4473360, 8937474, 811538, 9446947, 9701396, 9987093, 10226198, 10511895, 10751000, 11013657, 11298842,
     11538459, 7625244, 12063285, 8150558, 16818186, 21239350, 17350721, 21502007, 17875523, 18130445, 3705912,
     18655330, 134217328, 134217727, 134217727, 134217727, 134217727, 134217727, 134217727, 134217727, 134217727,
     134217727, 134217727, 134217727, 134217727, 134217727, 134217727, 134217727, 134217727, 134217727, 134217727,
     134217727, 134217727, 134217727, 134217727, 134217727, 134217727, 134217727, 134217727, 134217727, 134217727,
     134217727, 134217727, 134217727, 134217727, 134217727, 134217727, 134217727, 134217727, 134217727, 134217727,
     134217727, 134217727, 134217727, 134217727, 134217727, 22311439, 29666403, 134217727, 134217727, 134217727,
     134217727, 134217727, 134014024, 134217727, 134217727, 134217727, 134217727, 134217727, 134217727, 30191162,
     134217727, 134217727, 134217727, 134217727, 134217727, 134217727, 15511652, 30454345, 134217727, 134217727,
     134217727, 134217727, 134217727, 15774837, 133993573, 134217727, 134217727, 134217727, 134217727, 134217727,
     30964315, 24149067, 19970662, 134217727, 134217727, 134217727, 134217727, 16554615, 20500062, 134217727,
     134217727, 134217727, 134217727, 134217727, 27324511, 134217295, 134217727, 134217727, 134217727, 134217727,
     134217727, 134017641, 134217727, 134217727, 134217727, 134217727, 134217727, 134217727, 134018154, 134217727,
     134217727, 134217727, 134217727, 134217727, 134217727, 134018667, 134217727, 134217727, 134217727, 134217727,
     134217727, 134217727, 134019180, 134217727, 134217727, 134217727, 134217727, 134217727, 134217727, 134019693,
     134217727, 134217727, 134217727, 134217727, 134217727, 134217727, 33087086, 134217727, 134217727, 134217727,
     134217727, 134217727, 134217727, 134217343, 134217727, 134217727, 134217727, 134217727, 134217727, 134217727),
    (33554944, 33832976, 541201, 4785200, 811554, 9184899, 5310514, 34867236, 13388309, 9972870, 6098437, 13721639,
     6361328, 46402600, 10760841, 1958592, 11023498, 36529205, 50615835, 36704498, 14178332, 7674547, 47190573,
     37348919, 37510174, 2645535, 37873845, 50888784, 38016568, 47743569, 17376501, 21545143, 15068172, 51152531,
     17901665, 15298573, 39102199, 25784901, 3706006, 48789240, 18689620, 22382607, 15786136, 65352379, 18918499,
     49362033, 16070394, 22857917, 65856585, 23169692, 49866397, 41464382, 50198644, 16596581, 54585930, 41989373,
     42251974, 30971646, 42514641, 26846463, 134070435, 134217727, 134217727, 134217727, 134217727, 134217727,
     134217727, 134217727, 24440396, 59084452, 134217727, 134217727, 134217727, 134217727, 134217727, 27109029,
     31496798, 134071462, 134217727, 134217727, 134217727, 134217727, 43826900, 134217443, 134217727, 134217727,
     134217727, 134217727, 134217727, 31759573, 52514920, 56185449, 59831375, 134217727, 134217727, 134217727,
     56448106, 32331371, 134073033, 134217727, 134217727, 134217727, 134217727, 32594028, 45406936, 60396669,
     134217727, 134217727, 134217727, 134217727, 33119342, 134074073, 134217727, 134217727, 134217727, 134217727,
     134217727, 33381999, 134074571, 134217727, 134217727, 134217727, 134217727, 134217727, 134075098, 134217727,
     134217727, 134217727, 134217727, 134217727, 134217727, 134075596, 134217727, 134217727, 134217727, 134217727,
     134217727, 134217727, 57530061, 134217727, 134217727, 134217727, 134217727, 134217727, 134217727, 134076636,
     134217727, 134217727, 134217727, 134217727, 134217727, 134217727, 58055374, 134217727, 134217727, 134217727,
     134217727, 134217727, 134217727, 58302190, 134217727, 134217727, 134217727, 134217727, 134217727, 134217727,
     134078175, 134217727, 134217727, 134217727, 134217727, 134217727, 134217727),
    (4194816, 8659488, 4743170, 33579554, 9184771, 9447553, 1074306, 9710256, 5857923, 1378342, 6127667, 46729767,
     1593368, 6652550, 35416105, 6819507, 35774506, 11286196, 2167349, 47470620, 7673073, 2458669, 12074123,
     63466678, 12336780, 36967607, 51150928, 2911987, 37257809, 37520568, 25290937, 17569874, 48832568, 17875701,
     3508369, 38308435, 15068347, 49340500, 22289555, 18446996, 25697905, 39089399, 29928645, 65109142, 39614039,
     18710131, 23119512, 54556788, 23409401, 40471669, 23721021, 31012561, 18925630, 31323858, 16561820, 52247292,
     66359900, 24487582, 55656056, 19446885, 55967392, 66667129, 19709640, 134070434, 134217727, 134217727,
     134217727, 134217727, 32034006, 27111075, 52774988, 43316840, 59298520, 53038157, 59045994, 134217727,
     134217727, 134217727, 134217727, 134217727, 134217727, 134217727, 28153511, 44080253, 44357849, 28638412,
     59618474, 134217727, 134217727, 33332846, 59873963, 134217727, 134217727, 134217727, 134217727, 134217727,
     57497711, 134217445, 134217727, 134217727, 134217727, 134217727, 134217727, 45718701, 134073564, 134217727,
     134217727, 134217727, 134217727, 134217727, 54353629, 134217447, 134217727, 134217727, 134217727, 134217727,
     134217727, 60931806, 134217727, 134217727, 134217727, 134217727, 134217727, 134217727, 134217449, 134217727,
     134217727, 134217727, 134217727, 134217727, 134217727, 134075627, 134217727, 134217727, 134217727, 134217727,
     134217727, 134217727, 134217727, 134217727, 134217727, 134217727, 134217727, 134217727, 134217727, 134217452,
     134217727, 134217727, 134217727, 134217727, 134217727, 134217727, 134217453, 134217727, 134217727, 134217727,
     134217727, 134217727, 134217727, 134217454, 134217727, 134217727, 134217727, 134217727, 134217727, 134217727,
     134217455, 134217727, 134217727, 134217727, 134217727, 134217727, 134217727),
    (8389120, 4473360, 8937474, 46162450, 4998659, 9462961, 33652756, 5523972, 33907763, 50605094, 13698053,
     46935591, 10608771, 47189016, 6574724, 63269429, 11013765, 35226650, 47724075, 11538674, 48000028, 7625351,
     2459191, 12183176, 36007966, 63979055, 36270602, 14712912, 36443834, 51413585, 36825657, 25261634, 36968530,
     49409091, 15239265, 3504782, 64784979, 3771023, 18393278, 37875771, 50126946, 4006485, 38400720, 15786567,
     25996486, 38566514, 65580753, 30254228, 39091272, 30453959, 55389435, 39629412, 23625428, 66120265, 31011029,
     40210685, 66622555, 26555606, 66907740, 24458967, 19775689, 56703096, 41209057, 52992094, 27081849, 53331039,
     56966733, 134037731, 53517416, 134217377, 134217727, 134217727, 134217727, 134217727, 134217727, 32093289,
     42584143, 134217727, 134217727, 134217727, 134217727, 134217727, 60136042, 134217379, 134217727, 134217727,
     134217727, 134217727, 134217727, 57472619, 134217380, 134217727, 134217727, 134217727, 134217727, 134217727,
     54065260, 134217381, 134217727, 134217727, 134217727, 134217727, 134217727, 57735789, 33086694, 134217382,
     134217727, 134217727, 134217727, 134217727, 33349341, 134041319, 134217727, 134217727, 134217727, 134217727,
     134217727, 44159183, 134217727, 134217727, 134217727, 134217727, 134217727, 134217727, 58544862, 134217449,
     134217727, 134217727, 134217727, 134217727, 134217727, 134075562, 134217727, 134217727, 134217727, 134217727,
     134217727, 134217727, 134076075, 134217727, 134217727, 134217727, 134217727, 134217727, 134217727, 134076588,
     134217727, 134217727, 134217727, 134217727, 134217727, 134217727, 62217389, 134217727, 134217727, 134217727,
     134217727, 134217727, 134217727, 134077615, 134217727, 134217727, 134217727, 134217727, 134217727, 134217727,
     134217455, 134217727, 134217727, 134217727, 134217727, 134217727, 134217727),
    (4194816, 8659488, 8922114, 811568, 62932499, 63195156, 9710084, 5832754, 1434662, 10235521, 6416048, 13372456,
     10760834, 1960113, 13653018, 11286147, 34728626, 11548680, 11811574, 34869939, 12074231, 47284277, 2645535,
     50662648, 35422288, 2976505, 14189137, 17350792, 65542326, 35948114, 17875707, 14424759, 36211283, 48270588,
     22070286, 14809794, 36495431, 66592441, 26024021, 29666490, 51248781, 29913672, 58793047, 26310259, 59019864,
     30454415, 38084666, 30767330, 15563354, 23893093, 38389366, 15825995, 59844188, 19970662, 31293124, 60062285,
     41991376, 134217727, 134217727, 134217727, 134217727, 134217727, 134217727, 134217727, 134217727, 134217727,
     134217727, 134217727, 38837351, 24935654, 54849685, 134038079, 134217727, 134217727, 134217727, 20762855,
     134038738, 134217727, 134217727, 134217727, 134217727, 134217727, 51704425, 27870952, 134063738, 134217727,
     134217727, 134217727, 134217727, 28126953, 61418619, 32561316, 134217428, 134217727, 134217727, 134217727,
     28658411, 134064765, 134217727, 134217727, 134217727, 134217727, 134217727, 28914412, 33151640, 56155814,
     134057198, 134217727, 134217727, 134217727, 43900631, 44105432, 56971930, 44676251, 57497244, 134057644,
     134217727, 41269421, 41508061, 41794735, 134058207, 134217727, 134217727, 134217727, 134217417, 134217727,
     134217727, 134217727, 134217727, 134217727, 134217727, 134217418, 134217727, 134217727, 134217727, 134217727,
     134217727, 134217727, 134217419, 134217727, 134217727, 134217727, 134217727, 134217727, 134217727, 134217420,
     134217727, 134217727, 134217727, 134217727, 134217727, 134217727, 134217421, 134217727, 134217727, 134217727,
     134217727, 134217727, 134217727, 134217422, 134217727, 134217727, 134217727, 134217727, 134217727, 134217727,
     134217423, 134217727, 134217727, 134217727, 134217727, 134217727, 134217727),
    (8389120, 4473360, 4736002, 811568, 33564195, 33826852, 5523972, 10084402, 1377302, 6049521, 10552883, 63441944,
     34615849, 11013808, 13755930, 34879019, 50335921, 35141676, 7625460, 64324105, 12127797, 64578590, 2637359,
     21063304, 64777280, 17080843, 65104009, 21545026, 50926604, 14545475, 47482977, 47717003, 65571411, 25790092,
     3798598, 18655288, 4004535, 66117717, 37821497, 18918499, 37616241, 15299256, 19181156, 38141042, 15829051,
     66905688, 23362234, 38387828, 19430501, 38631029, 49315418, 31048283, 24193099, 49597666, 31277205, 51690060,
     39437985, 24694434, 59830349, 24987326, 43069119, 27325006, 43331813, 134062185, 134217727, 134217727,
     134217727, 134217727, 20794566, 60347514, 28135065, 60634235, 32561320, 134217425, 134217727, 134217426,
     134217727, 134217727, 134217727, 134217727, 134217727, 134217727, 32823977, 44683419, 40959086, 29185769,
     134063743, 134217727, 134217727, 52254954, 134217428, 134217727, 134217727, 134217727, 134217727, 134217727,
     61684397, 61947054, 134064815, 134217727, 134217727, 134217727, 134217727, 56180461, 134217727, 134217727,
     134217727, 134217727, 134217727, 134217727, 52813000, 134065903, 134217727, 134217727, 134217727, 134217727,
     134217727, 134217432, 134217727, 134217727, 134217727, 134217727, 134217727, 134217727, 53327050, 134217433,
     134217727, 134217727, 134217727, 134217727, 134217727, 134217727, 134217727, 134217727, 134217727, 134217727,
     134217727, 134217727, 53844188, 134217435, 134217727, 134217727, 134217727, 134217727, 134217727, 134217727,
     134217727, 134217727, 134217727, 134217727, 134217727, 134217727, 54369502, 134217437, 134217727, 134217727,
     134217727, 134217727, 134217727, 134217727, 134217727, 134217727, 134217727, 134217727, 134217727, 134217727,
     134217439, 134217727, 134217727, 134217727, 134217727, 134217727, 134217727),
    (8389120, 4473360, 8937474, 811538, 13116963, 1058852, 5524019, 5786752, 13697541, 46149159, 62926888, 10814470,
     50422297, 1862385, 34354218, 7100146, 2164929, 11625526, 11920924, 14509597, 12126729, 35252254, 47201839,
     21096970, 47476800, 35395266, 17080889, 17371382, 21545142, 17690124, 25498307, 15298116, 18130445, 22091000,
     3764336, 22409787, 29658256, 4003513, 65566818, 22616209, 51475570, 16035579, 66132595, 26027079, 37283928,
     66418238, 38595161, 49329295, 26274964, 66616904, 39190135, 51739227, 49844828, 39383133, 26554080, 50107486,
     59060345, 40146527, 134037712, 134217727, 134217727, 134217727, 134217727, 134217727, 134217727, 134217727,
     134217727, 134217727, 51967078, 27116753, 55129164, 134217377, 134217727, 134217727, 134217727, 40695400,
     134038755, 134217727, 134217727, 134217727, 134217727, 134217727, 20265065, 134039251, 134217727, 134217727,
     134217727, 134217727, 134217727, 52230250, 28166356, 20527741, 134039765, 134217727, 134217727, 134217727,
     56179820, 28638373, 134072991, 134217727, 134217727, 134217727, 134217727, 20765862, 56426184, 52747943,
     134073560, 134217727, 134217727, 134217727, 44151498, 134074059, 134217727, 134217727, 134217727, 134217727,
     134217727, 57252009, 57514666, 134217448, 134217727, 134217727, 134217727, 134217727, 134075086, 134217727,
     134217727, 134217727, 134217727, 134217727, 134217727, 45201579, 61462223, 134217727, 134217727, 134217727,
     134217727, 134217727, 134217727, 134217727, 134217727, 134217727, 134217727, 134217727, 134217727, 58284765,
     45996718, 134076639, 134217727, 134217727, 134217727, 134217727, 134217727, 134217727, 134217727, 134217727,
     134217727, 134217727, 134217727, 134077679, 134217727, 134217727, 134217727, 134217727, 134217727, 134217727,
     134217727, 134217727, 134217727, 134217727, 134217727, 134217727, 134217727),
    (4194816, 8659488, 8922114, 811568, 13125139, 1067028, 9710256, 9972976, 46402099, 10235633, 6357044, 63441960,
     10760882, 1862273, 63722522, 7144627, 2222123, 11548864, 34368692, 2382365, 64318145, 14441502, 8252548,
     47715375, 16818309, 21239543, 48001089, 17428614, 21545017, 17662988, 25522425, 3477060, 18130568, 15299322,
     3740355, 48794708, 65855586, 36206165, 49149967, 15786567, 37878358, 22864995, 30242955, 49675409, 36745288,
     30440077, 51425892, 49839359, 30708314, 31047826, 37584526, 19474011, 54641215, 31242341, 54903956, 19737181,
     59614328, 55364805, 39360606, 59877497, 39632487, 39955021, 27372773, 56462414, 32099433, 56701519, 134037610,
     134217727, 28160666, 42323579, 134217727, 134217727, 134217727, 134217727, 134217727, 60881004, 28685467,
     134038653, 134217727, 134217727, 134217727, 134217727, 33086620, 57511657, 61406831, 134217379, 134217727,
     134217727, 134217727, 134217380, 134217727, 134217727, 134217727, 134217727, 134217727, 134217727, 61684444,
     61979294, 62241951, 134217381, 134217727, 134217727, 134217727, 134040799, 134217727, 134217727, 134217727,
     134217727, 134217727, 134217727, 52813000, 44143855, 134217383, 134217727, 134217727, 134217727, 134217727,
     134217727, 134217727, 134217727, 134217727, 134217727, 134217727, 134217727, 53581482, 134042284, 134217727,
     134217727, 134217727, 134217727, 134217727, 134217727, 134217727, 134217727, 134217727, 134217727, 134217727,
     134217727, 54090957, 134217387, 134217727, 134217727, 134217727, 134217727, 134217727, 134217727, 134217727,
     134217727, 134217727, 134217727, 134217727, 134217727, 134044367, 134217727, 134217727, 134217727, 134217727,
     134217727, 134217727, 134217727, 134217727, 134217727, 134217727, 134217727, 134217727, 134217727, 134217391,
     134217727, 134217727, 134217727, 134217727, 134217727, 134217727),
)
NF = F // NC
ROWS = ('E3', 'E1', 'P0', 'P1', 'E2', 'P3', 'P2')
ITEMS = ('own', *ROWS, *sorted(NAMES.values()))
PIECE = {n: p for p, n in NAMES.items()}


def whiten(spectra, quality, put):
    here = lax.broadcasted_iota(jnp.int32, (CH, CH), 0) == lax.broadcasted_iota(jnp.int32, (CH, CH), 1)
    usable = jnp.sum(jnp.where(here, quality[...].astype(jnp.float32), 0.0), axis=1, keepdims=True)

    def parts(f):
        values = spectra[f].astype(jnp.float32)
        real_part, imag_part = values[:, :W], values[:, W:]
        return real_part, imag_part, real_part * real_part + imag_part * imag_part

    def add(f, total):
        return total + parts(f)[2]

    mean_energy = lax.fori_loop(0, F, add, jnp.zeros((CH, W), jnp.float32), unroll=4) / F

    def scale(f, carry):
        real_part, imag_part, energy = parts(f)
        factor = usable / jnp.sqrt(energy + mean_energy + 1e-06)
        put(f, jnp.concatenate([real_part * factor, imag_part * factor], axis=1).astype(jnp.bfloat16))
        return carry

    lax.fori_loop(0, F, scale, 0, unroll=4)


def any_of(q, places):
    hit = q < 0
    for place in places:
        hit = hit | (q == place)
    return hit


def gather_kernel(spectra, quality, cross, rowb, colb, steps, local_sem, row_sem, col_sem, sib_sem, srow_sem, sr_sem,
                  scol_sem, ssib_sem):
    row, col = lax.axis_index("row"), lax.axis_index("col")
    core, x, y_lo = row % 2, (row // 2) % 4, row // 8
    z, y_hi = col // 2, col % 2
    y = y_hi * 2 + y_lo

    def at(xx, yy, zz, cc):
        return {"row": (yy % 2) * 8 + xx * 2 + cc, "col": zz * 2 + yy // 2}

    x_up, x_dn = at((x + 1) % 4, y, z, core), at((x + 3) % 4, y, z, core)
    z_up, z_dn = at(x, y, (z + 1) % 4, core), at(x, y, (z + 3) % 4, core)
    sibling = at(x, y, z, 1 - core)
    partner = at(x, (y + 2) % 4, z, core)
    pair = at(x, y_hi * 2 + 1 - y_lo, z, core)
    other = at(x, (y + 3 + 2 * y_lo) % 4, z, core)

    q = (x + 4 - col % 4) % 4
    mirror = (y_lo + 2 - col // 4) % 2
    place = mirror * 4 + q
    k = y_lo * 4 + x
    is_root = k == col
    not_root = jnp.logical_not(is_root)
    feeds = (z == k // 2) & (y_hi != k % 2)

    def ident(piece):
        half = y_hi if piece[0] == 'E' else 1 - y_hi
        return ((z + int(piece[1])) % 4) * 2 + half

    ids = {p: ident(p) for p in NAMES}

    def chunk(g):
        return pl.ds(g * NF, NF)

    def remote(src, dst, send, recv, to):
        pltpu.make_async_remote_copy(src, dst, send, recv, device_id=to, device_id_type=MESH).start()

    def row_send(slot, piece, g, to):
        part = rowb.at[ids[piece], chunk(g)]
        remote(part, part, srow_sem.at[slot], row_sem.at[ids[piece], g], to)

    def col_send(src, slot, way, piece, g, to):
        dst = colb.at[core * 8 + ids[piece], chunk(g)]
        remote(dst if src is None else src, dst, scol_sem.at[slot, way], col_sem.at[ids[piece], g], to)

    def done(ref, sem):
        pltpu.make_async_copy(ref, ref, sem).wait()

    slots = {n: i for i, n in enumerate(PIECE)}
    barrier = pltpu.get_barrier_semaphore()
    for peer in (x_up, x_dn, pair, other, z_up, z_dn, sibling, partner):
        pl.semaphore_signal(barrier, inc=1, device_id=peer, device_id_type=MESH)

    def put(f, values):
        rowb[ids['E0'], f] = values

    whiten(spectra, quality, put)
    pl.semaphore_wait(barrier, 8)

    def root_step(piece, g):
        name = NAMES[piece]
        src = rowb.at[ids[piece], chunk(g)]
        if name[0] == 'a':
            col_send(src, slots[name], 0, piece, g, x_up)
        if name[0] == 'b':
            col_send(src, slots[name], 1, piece, g, x_dn)

    def first(g, carry):
        row_send(0, 'E0', g, z_up)
        row_send(1, 'E0', g, z_dn)

        @pl.when(is_root)
        def _():
            root_step('E0', g)

        return carry

    lax.fori_loop(0, NC, first, 0)
    for i in range(len(ORDER[0])):
        word = jnp.int32(ORDER[0][i])
        for p in range(1, 8):
            word = jnp.where(place == p, ORDER[p][i], word)
        steps[i] = word

    def y_own(g):
        row_send(6, 'E0', g, partner)

    feed_slot = {'E' + PIECE[n][1]: i for i, n in enumerate(('y0', 'y1'))}

    def row_step(piece, g):
        done(rowb.at[ids[piece], chunk(g)], row_sem.at[ids[piece], g])
        if piece == 'E3':
            row_send(2, piece, g, z_up)
        if piece == 'P0':
            row_send(3, piece, g, z_up)
            row_send(4, piece, g, z_dn)
        if piece == 'P1':
            row_send(5, piece, g, z_dn)

        @pl.when(is_root)
        def _():
            root_step(piece, g)

        if piece in feed_slot:
            @pl.when(feeds)
            def _():
                dst = colb.at[core * 8 + ids[piece], chunk(g)]
                remote(rowb.at[ids[piece], chunk(g)], dst, sr_sem.at[feed_slot[piece]], col_sem.at[ids[piece], g], other)

    on_root_row = mirror == 0
    ways = {}
    for name in slots:
        up = on_root_row & any_of(q, (1, 2)) & (name[0] == 'a')
        down = on_root_row & any_of(q, (3, 2)) & (name[0] == 'b')
        over = jnp.where(on_root_row, any_of(q, [p for p in (1, 2, 3) if name in ENTRY[p]]),
                         any_of(q, (1, 2, 3)) & (name[0] == 'y'))
        enters = [p for p in range(4) if name in ENTRY[p]][0]
        order = ENTRY[enters].index(name)
        mirrored = mirror == 1
        full = mirrored & (q == enters)
        up_half = mirrored & (q == (enters + 1) % 4)
        down_half = mirrored & (q == (enters + 3) % 4)
        ways[name] = (up | full, up_half, down | full, down_half, over, order)

    def col_step(name, g):
        piece = PIECE[name]
        slot = slots[name]
        done(colb.at[core * 8 + ids[piece], chunk(g)], col_sem.at[ids[piece], g])
        up, up_half, down, down_half, over, order = ways[name]

        @pl.when(up | (up_half & (g % 2 == order)))
        def _():
            col_send(None, slot, 0, piece, g, x_up)

        @pl.when(down | (down_half & (g % 2 != order)))
        def _():
            col_send(None, slot, 1, piece, g, x_dn)

        @pl.when(over)
        def _():
            col_send(None, slot, 2, piece, g, pair)

    my_half = colb.at[pl.ds(core * 8, 8)]

    def swap(g):
        mine = my_half.at[:, chunk(g)]

        @pl.when(is_root)
        def _():
            pltpu.make_async_copy(rowb.at[:, chunk(g)], mine, local_sem.at[g]).start()
            remote(rowb.at[:, chunk(g)], mine, ssib_sem, sib_sem.at[g], sibling)

        @pl.when(not_root)
        def _():
            remote(mine, mine, ssib_sem, sib_sem.at[g], sibling)

    def multiply(g):
        @pl.when(is_root)
        def _():
            done(my_half.at[:, chunk(g)], local_sem.at[g])

        done(my_half.at[:, chunk(g)], sib_sem.at[g])

        def two_bins(h, carry):
            parts = []
            for e in range(2):
                f = g * NF + h * 2 + e
                lhs = rowb[:, f].reshape(8 * CH, 2 * W)
                turned = jnp.concatenate([lhs[:, W:], -lhs[:, :W]], axis=1)
                rhs = colb[:, f].reshape(16 * CH, 2 * W)
                parts.append(lax.dot_general(jnp.concatenate([lhs, turned], axis=0), rhs, (((1,), (1,)), ((), ())),
                                             preferred_element_type=jnp.float32))
            for c in range(2):
                both = [p[c * 256:(c + 1) * 256].reshape(32, 8, 512) for p in parts]
                cross[c, :, g * (NF // 2) + h] = jnp.concatenate(both, axis=1).astype(jnp.bfloat16)
            return carry

        lax.fori_loop(0, NF // 2, two_bins, 0)

    acts = [functools.partial(row_step, n) if n in ROWS else functools.partial(col_step, n) if n in PIECE
            else y_own for n in ITEMS]

    def choose(item, g, low, high):
        if high - low == 1:
            acts[low](g)
            return
        middle = (low + high) // 2

        @pl.when(item < middle)
        def _():
            choose(item, g, low, middle)

        @pl.when(item >= middle)
        def _():
            choose(item, g, middle, high)

    def three(i, carry):
        def one(_, word):
            step = lax.rem(word, 512)
            item, g = lax.div(step, 16), lax.rem(step, 16)

            @pl.when(item < len(ITEMS))
            def _():
                choose(item, g, 0, len(ITEMS))

            return lax.div(word, 512)

        lax.fori_loop(0, 3, one, steps[i])
        return carry

    lax.fori_loop(0, BEFORE, three, 0)

    swap(0)

    def with_multiply(g, carry):
        start = BEFORE + g * BETWEEN
        lax.fori_loop(start, start + BETWEEN, three, 0)
        swap(g + 1)
        multiply(g)
        return carry

    lax.fori_loop(0, NC - 1, with_multiply, 0)
    multiply(NC - 1)

    whole = rowb.at[0]
    half_piece = rowb.at[0, pl.ds(0, F // 2)]
    for i in range(7):
        done(whole, srow_sem.at[i])

    @pl.when(feeds)
    def _():
        done(whole, sr_sem.at[0])
        done(whole, sr_sem.at[1])

    for name in slots:
        up, up_half, down, down_half, over, _ = ways[name]
        slot = slots[name]
        for way, full, part, letter in ((0, up, up_half, 'a'), (1, down, down_half, 'b')):
            @pl.when(jnp.where(is_root, name[0] == letter, full))
            def _(slot=slot, way=way):
                done(whole, scol_sem.at[slot, way])

            @pl.when(not_root & part)
            def _(slot=slot, way=way):
                done(half_piece, scol_sem.at[slot, way])

        @pl.when(not_root & over)
        def _(slot=slot):
            done(whole, scol_sem.at[slot, 2])


    done(my_half, ssib_sem)


def gather_cross(spectra, quality):
    piece = (F, CH, 2 * W)
    vmem = pl.BlockSpec(memory_space=pltpu.VMEM)
    return pl.pallas_call(
        gather_kernel,
        out_shape=pltpu.VMEM((2, 32, F // 2, 16, 512), jnp.bfloat16),
        in_specs=[vmem, vmem],
        out_specs=vmem,
        scratch_shapes=[
            pltpu.VMEM((8, *piece), jnp.bfloat16),
            pltpu.VMEM((16, *piece), jnp.bfloat16),
            pltpu.SMEM((len(ORDER[0]),), jnp.int32),
            pltpu.SemaphoreType.DMA((NC,)),
            pltpu.SemaphoreType.DMA((8, NC)),
            pltpu.SemaphoreType.DMA((8, NC)),
            pltpu.SemaphoreType.DMA((NC,)),
            pltpu.SemaphoreType.DMA((7,)),
            pltpu.SemaphoreType.DMA((2,)),
            pltpu.SemaphoreType.DMA((8, 3)),
            pltpu.SemaphoreType.DMA,
        ],
        compiler_params=pltpu.CompilerParams(collective_id=0, has_side_effects=True, vmem_limit_bytes=40 << 20),
        name="gather_cross",
    )(spectra, quality.reshape(1, CH))


def lag_matrices():
    lag = np.arange(HALF + 1, dtype=np.float32)
    frequency = np.arange(F, dtype=np.float32) + np.float32(1.0)
    angles = np.float32(2.0 * math.pi) * frequency[None, :] * lag[:, None] / np.float32(2.0 * LAGS)
    eye = np.eye(8, dtype=np.float32)
    return [np.kron(m, eye).astype(jnp.bfloat16) for m in (np.cos(angles), -np.sin(angles))]


def lag_kernel(mask, cross, even_mat, odd_mat, out, buf, sem):
    rows, cols = out.shape[1], out.shape[2]
    wide = 256
    tile_row = lax.axis_index("row") * (rows // BLK)
    tile_col = lax.axis_index("col") * (cols // BLK)

    def copy(step):
        here = pl.ds(pl.multiple_of(step * 16, 16), 16)
        return pltpu.make_async_copy(buf.at[:, here], out.at[:, here], sem.at[step])

    def one(step, carry):
        here = pl.ds(pl.multiple_of(step * 16, 16), 16)
        for j in range(cols // wide):
            span = slice(j * wide, (j + 1) * wide)
            scale = jnp.concatenate(
                [jnp.full((1, BLK), mask[tile_row + step // 8, tile_col + t].astype(jnp.float32)
                          * (1.0 / math.sqrt(W * F)), jnp.float32)
                 for t in range(j * wide // BLK, (j + 1) * wide // BLK)], axis=1)
            even, odd = [], []
            for h in range(2):
                at = step * 2 + h
                even.append(jnp.dot(even_mat[...], cross[0, at, :, :, span].reshape(F * 8, wide),
                                    preferred_element_type=jnp.float32))
                odd.append(jnp.dot(odd_mat[...], cross[1, at, :, :, span].reshape(F * 8, wide),
                                   preferred_element_type=jnp.float32))
            for m in range(HALF + 1):
                e = [v[m * 8:m * 8 + 8] for v in even]
                o = [v[m * 8:m * 8 + 8] for v in odd]
                if m < HALF:
                    buf[HALF + m, here, span] = (
                        jnp.concatenate([a + b for a, b in zip(e, o)], 0) * scale).astype(out.dtype)
                if m > 0:
                    buf[HALF - m, here, span] = (
                        jnp.concatenate([a - b for a, b in zip(e, o)], 0) * scale).astype(out.dtype)
        copy(step).start()
        return carry

    lax.fori_loop(0, rows // 16, one, 0, unroll=4)

    def finish(step, carry):
        copy(step).wait()
        return carry

    lax.fori_loop(0, rows // 16, finish, 0)


def lag_transform(cross, tile_mask):
    rows, cols = 256, 512
    even_mat, odd_mat = lag_matrices()
    vmem = pl.BlockSpec(memory_space=pltpu.VMEM)
    return pl.pallas_call(
        lag_kernel,
        in_specs=[pl.BlockSpec(memory_space=pltpu.SMEM), vmem, vmem, vmem],
        out_specs=pl.BlockSpec(memory_space=pl.ANY),
        out_shape=jax.ShapeDtypeStruct((LAGS, rows, cols), jnp.bfloat16),
        scratch_shapes=[pltpu.VMEM((LAGS, rows, cols), jnp.bfloat16), pltpu.SemaphoreType.DMA((rows // 16,))],
        compiler_params=pltpu.CompilerParams(vmem_limit_bytes=30 << 20),
        name="lag_transform",
    )(tile_mask, cross, even_mat, odd_mat)


def per_device(spectra, quality, tile_mask):
    cross = gather_cross(spectra, quality)
    return lag_transform(cross, tile_mask)


def solution(mesh):
    placed = (P(None, ("row", "col"), None), P(("row", "col")), P())
    return jax.shard_map(
        per_device, mesh=mesh, in_specs=placed, out_specs=P(None, "row", "col"), check_vma=False
    )
```
